32 devices in a mesh: ctx: 8 (over y, x, core), tp: 4 (over z).
Axes of the slice: x: 2, y: 2, z: 4, core: 2. Of those that a mesh axis runs over, the one named last changes fastest.
Arguments:
- queries: bfloat16 [4096, 32, 128], P('ctx', 'tp'), may hold values from -110 to 110
- keys: bfloat16 [4096, 32, 128], P('ctx', 'tp'), may hold values from -7 to 7
- values: bfloat16 [4096, 32, 128], P('ctx', 'tp'), may hold values from -6 to 6
- seg_lengths: int32 [256], replicated, may hold values from 1 to 32, 4096 in all
- out_weight: bfloat16 [4096, 4096], P('tp'), may hold values from -0.09375 to 0.09375
Outputs:
- mixed: bfloat16 [4096, 4096], P('ctx', 'tp')
The draws below stay inside these ranges and needn't reach their ends.
Inputs may be any that keep to these rules, and one draw needn't show every extreme that they name: `seg_lengths`: the 256 segment lengths sum to 4096; the longest is exactly 32.
All inputs are finite; a program needn't handle non-finite values.
Results may differ from the reference program's by a relative error of at most 0.039.
Values may be sent and summed in bfloat16 or wider, within the bound.
A program may use at most 128 MiB of HBM per device.

```python
import math
import jax
import jax.numpy as jnp
import numpy as np
from jax import lax

D = 4096
HEADS = 32
HD = 128
M = 256
ITERS = 6
TOK_DEV = 512
TOKENS = 4096
SEG_MOST = 32
N_TP = 4


def draw_together(key):
    query_key = jax.random.fold_in(key, 11)
    key_key = jax.random.fold_in(key, 12)
    shape = (TOKENS, HEADS, HD)
    key_rows = jax.random.truncated_normal(key_key, -5.0, 5.0, shape, jnp.float32)
    query_rows = jax.random.truncated_normal(query_key, -5.0, 5.0, shape, jnp.float32)
    return (query_rows, key_rows)


def draw_queries(key, part):
    return draw_together(key)[0].astype(jnp.bfloat16)


def draw_keys(key, part):
    return draw_together(key)[1].astype(jnp.bfloat16)


def block_levels(rng, shape, cuts, smallest, high):
    loudness, own = 1.0, jax.random.fold_in(rng, 6)
    for dim, blocks in cuts:
        draws = jnp.exp(jax.random.uniform(jax.random.fold_in(own, dim), (blocks,), jnp.float32, smallest / len(cuts), high / len(cuts)))
        loudness = loudness * jnp.repeat(draws, shape[dim] // blocks).reshape([-1 if axis == dim else 1 for axis in range(len(shape))])
    return loudness


def profile(amount, total, most, skew):
    weights = [(1 << 20) // math.isqrt(standing ** skew) + 1 for standing in range(2, amount + 1)]
    spare, counts = total - most - (amount - 1), [1] * (amount - 1)
    while spare > 0:
        candidates = [i for i in range(amount - 1) if counts[i] < most]
        mass, budget = sum([weights[i] for i in candidates]), spare
        for i in candidates:
            addition = min(most - counts[i], max(1, budget * weights[i] // mass), spare)
            counts[i] = counts[i] + addition
            spare = spare - addition
    return np.array([most] + counts)


def ragged_sizes(rng, number_of, total, most, lean):
    if number_of == 2:
        one = jax.random.randint(rng, (), max(1, total - most), min(most, total - 1) + 1)
        return jnp.stack([one, total - one])
    sizes = jnp.asarray(profile(number_of, total, most, lean), jnp.int32)
    twos = (number_of - 1) // 2
    donor, taker = sizes[1:1 + 2 * twos:2], sizes[2:2 + 2 * twos:2]
    slack = jnp.minimum(donor - 1, most - taker)
    passed = jax.random.randint(jax.random.fold_in(rng, 1), (twos,), 0, 1 << 20) % (slack + 1)
    sizes = sizes.at[1:1 + 2 * twos:2].set(donor - passed).at[2:2 + 2 * twos:2].set(taker + passed)
    return sizes[jax.random.permutation(jax.random.fold_in(rng, 2), number_of)]


def centred(rng, extent, deviation, limit, cuts=(), kind=jnp.bfloat16):
    drawn = deviation * jax.random.normal(rng, extent, jnp.float32)
    if cuts:
        drawn = drawn * block_levels(rng, extent, cuts, -0.22, 0.18)
    return jnp.clip(drawn, -limit, limit).astype(kind)


def setup_inputs(seed: int = 0) -> dict:
    key_list = jax.random.split(jax.random.key(seed), 6)
    queries = draw_queries(jax.random.fold_in(key_list[5], 71), 0)
    keys = draw_keys(jax.random.fold_in(key_list[5], 71), 0)
    values = centred(key_list[2], (TOKENS, HEADS, HD), 1.0, 6.0, ((0, 8), (1, 4)))
    seg_lengths = ragged_sizes(key_list[3], M, TOKENS, SEG_MOST, 2).astype(jnp.int32)
    out_weight = centred(key_list[4], (HEADS * HD, D), (HEADS * HD) ** -0.5, 0.09375, ((0, 4),))
    return {"queries": queries, "keys": keys, "values": values, "seg_lengths": seg_lengths, "out_weight": out_weight}


very_negative = -1e+30

def cast_to_bfloat16(array):
    return lax.optimization_barrier(array.astype(jnp.bfloat16)).astype(jnp.float32)

def merge_states(earlier, latter):
    top_peak = jnp.maximum(earlier[0], latter[0])
    first_factor = jnp.exp(earlier[0] - top_peak)
    second_factor = jnp.exp(latter[0] - top_peak)
    return (top_peak, earlier[1] * first_factor + latter[1] * second_factor, earlier[2] * first_factor[..., None] + latter[2] * second_factor[..., None])

def masked_weights(scores, allowed):
    masked = jnp.where(allowed, scores, very_negative)
    top_score = lax.optimization_barrier(jnp.max(masked, axis=-1, keepdims=True))
    expo = jnp.where(allowed, jnp.exp(masked - top_score), 0.0)
    return expo / jnp.maximum(lax.optimization_barrier(jnp.sum(expo, axis=-1, keepdims=True)), 1.0)

def newton_inverse(attention_kernel):
    highest = lax.Precision.HIGHEST
    row_sum = lax.optimization_barrier(jnp.max(lax.optimization_barrier(jnp.sum(attention_kernel, axis=2)), axis=-1))
    col_sum = lax.optimization_barrier(jnp.max(lax.optimization_barrier(jnp.sum(attention_kernel, axis=1)), axis=-1))
    approx = jnp.swapaxes(attention_kernel, 1, 2) / (row_sum * col_sum)[:, None, None]
    identity = jnp.eye(attention_kernel.shape[-1], dtype=jnp.float32)
    for iteration in range(ITERS):
        applied = jnp.einsum('hij,hjk->hik', attention_kernel, approx, precision=highest)
        factor = 7.0 * identity - applied
        factor = 15.0 * identity - jnp.einsum('hij,hjk->hik', applied, factor, precision=highest)
        factor = 13.0 * identity - jnp.einsum('hij,hjk->hik', applied, factor, precision=highest)
        approx = 0.25 * jnp.einsum('hij,hjk->hik', approx, factor, precision=highest)
    return approx

def reference(queries, keys, values, seg_lengths, out_weight):
    score_scale_factor = HD ** (-0.5)
    seg_ends = jnp.cumsum(seg_lengths).astype(jnp.int32)
    seg_begins = seg_ends - seg_lengths
    position = jnp.arange(TOKENS, dtype=jnp.int32)
    block_member_mask = ((position[None, :] >= seg_begins[:, None]) & (position[None, :] < seg_ends[:, None])).astype(jnp.float32)
    seg_root = jnp.sqrt(seg_lengths.astype(jnp.float32))[None, :, None]
    query_block_sums = jnp.einsum('na,abf->bnf', block_member_mask, queries.astype(jnp.float32))
    key_block_sums = jnp.einsum('na,abf->bnf', block_member_mask, keys.astype(jnp.float32))
    landmark_query_rows = (query_block_sums / seg_root).astype(jnp.bfloat16).astype(jnp.float32)
    landmark_key_rows = (key_block_sums / seg_root).astype(jnp.bfloat16).astype(jnp.float32)
    attention_kernel = jax.nn.softmax(jnp.einsum('slu,szu->slz', landmark_query_rows, landmark_key_rows) * score_scale_factor, axis=-1)
    pseudo_inverse_matrix = newton_inverse(attention_kernel)
    blocks = TOKENS // TOK_DEV
    query_blocks = queries.reshape(blocks, TOK_DEV, HEADS, HD).astype(jnp.float32)
    key_blocks = keys.reshape(blocks, TOK_DEV, HEADS, HD).astype(jnp.float32)
    value_blocks = values.reshape(blocks, TOK_DEV, HEADS, HD).astype(jnp.float32)
    group_weight = out_weight.reshape(N_TP, HEADS // N_TP * HD, D).astype(jnp.float32)
    causal = jnp.arange(TOK_DEV)[:, None] >= jnp.arange(TOK_DEV)[None, :]

    def one_block(carry, inputs):
        query_block_rows, key_block_rows, value_block_rows, block_id = inputs
        block_start = block_id * TOK_DEV
        allowed = seg_ends <= block_start
        landmark_value_rows = jnp.where(allowed[None, :, None], carry[2] / jnp.maximum(carry[1], 1.0)[..., None], 0.0)
        blended_state = cast_to_bfloat16(jnp.einsum('bxz,bzl->bxl', pseudo_inverse_matrix, landmark_value_rows, precision=lax.Precision.HIGHEST))
        local_scores = jnp.einsum('thd,uhd->htu', query_block_rows, key_block_rows) * score_scale_factor
        local_scores = jnp.where(causal[None], local_scores, very_negative)
        local_probs = cast_to_bfloat16(jax.nn.softmax(local_scores, axis=-1))
        local_block_output = jnp.einsum('htu,uhd->thd', local_probs, value_block_rows)
        landmark_score_matrix = jnp.einsum('byz,yfz->ybf', query_block_rows, landmark_key_rows) * score_scale_factor
        landmark_weight_matrix = cast_to_bfloat16(masked_weights(landmark_score_matrix, allowed[None, None, :]))
        landmark_attention_layer = cast_to_bfloat16(local_block_output + jnp.einsum('ecp,epy->cey', landmark_weight_matrix, blended_state))
        grouped = landmark_attention_layer.reshape(TOK_DEV, N_TP, HEADS // N_TP * HD)
        partial_value = cast_to_bfloat16(jnp.einsum('tgk,gkd->gtd', grouped, group_weight))
        block_out = lax.optimization_barrier(jnp.sum(partial_value, axis=0)).astype(jnp.bfloat16)
        state_score_matrix = jnp.einsum('fcb,pfb->fcp', landmark_query_rows, key_block_rows) * score_scale_factor
        state_peak = lax.optimization_barrier(jnp.max(state_score_matrix, axis=-1))
        state_exponent = jnp.exp(state_score_matrix - state_peak[..., None])
        state_total = lax.optimization_barrier(jnp.sum(state_exponent, axis=-1))
        state_running_total = jnp.einsum('ogq,qoc->ogc', cast_to_bfloat16(state_exponent), value_block_rows)
        return (merge_states(carry, (state_peak, state_total, state_running_total)), block_out)
    start_state = (jnp.full((HEADS, M), very_negative, jnp.float32), jnp.zeros((HEADS, M), jnp.float32), jnp.zeros((HEADS, M, HD), jnp.float32))
    block_ids = jnp.arange(blocks, dtype=jnp.int32)
    final_state, outputs = lax.scan(one_block, start_state, (query_blocks, key_blocks, value_blocks, block_ids))
    return outputs.reshape(TOKENS, D)
```

```python
import functools

import jax
import jax.numpy as jnp
from jax import lax
from jax.experimental import pallas as pl
from jax.experimental.pallas import tpu as pltpu
from jax.sharding import PartitionSpec as P

ITERS = 6


very_negative = -1e30


def prefix(shard, axis, combine, identity):
    peers, index = (lax.axis_size(axis), lax.axis_index(axis))
    everything = jax.tree.map(
        lambda part, kind: lax.all_gather(part.astype(kind), axis),
        shard,
        (jnp.bfloat16, jnp.bfloat16, jnp.bfloat16),
    )
    start = jax.tree.map(
        lambda part, zero: jnp.broadcast_to(jnp.asarray(zero, part.dtype), part.shape),
        shard,
        identity,
    )

    def lap(k, before):
        reached = k < index
        new = combine(
            before, jax.tree.map(lambda part, own: part[k].astype(own.dtype), everything, shard)
        )
        return jax.tree.map(lambda a, b: jnp.where(reached, a, b), new, before)

    return lax.fori_loop(0, peers, lap, start)


def merge_states(earlier, latter):
    top_peak = jnp.maximum(earlier[0], latter[0])
    first_factor = jnp.exp(earlier[0] - top_peak)
    second_factor = jnp.exp(latter[0] - top_peak)
    return (
        top_peak,
        earlier[1] * first_factor + latter[1] * second_factor,
        earlier[2] * first_factor[..., None] + latter[2] * second_factor[..., None],
    )


def masked_weights(scores, allowed):
    masked = jnp.where(allowed, scores, very_negative)
    top_score = jnp.max(masked, axis=-1, keepdims=True)
    expo = jnp.where(allowed, jnp.exp(masked - top_score), 0.0)
    return expo / jnp.maximum(jnp.sum(expo, axis=-1, keepdims=True), 1.0)


def newton_inverse(attention_kernel):
    highest = lax.Precision.HIGHEST
    row_sum = jnp.max(jnp.sum(attention_kernel, axis=2), axis=-1)
    col_sum = jnp.max(jnp.sum(attention_kernel, axis=1), axis=-1)
    approx = jnp.swapaxes(attention_kernel, 1, 2) / (row_sum * col_sum)[:, None, None]
    identity = jnp.eye(attention_kernel.shape[-1], dtype=jnp.float32)
    for iteration in range(ITERS):
        applied = jnp.einsum("hij,hjk->hik", attention_kernel, approx, precision=highest)
        factor = 7.0 * identity - applied
        factor = 15.0 * identity - jnp.einsum("hij,hjk->hik", applied, factor, precision=highest)
        factor = 13.0 * identity - jnp.einsum("hij,hjk->hik", applied, factor, precision=highest)
        approx = 0.25 * jnp.einsum("hij,hjk->hik", approx, factor, precision=highest)
    return approx


def on_device(queries, keys, values, seg_lengths, out_weight):
    row_count, heads_here, head_dim = queries.shape
    landmarks = seg_lengths.shape[0]
    score_scale_factor = head_dim ** (-0.5)
    block_start = lax.axis_index("ctx") * row_count
    seg_ends = jnp.cumsum(seg_lengths)
    seg_begins = seg_ends - seg_lengths
    position = block_start + jnp.arange(row_count, dtype=jnp.int32)
    block_member_mask = (
        (position[None, :] >= seg_begins[:, None]) & (position[None, :] < seg_ends[:, None])
    ).astype(jnp.bfloat16)
    query_block_sums = jnp.einsum(
        "na,abf->bnf", block_member_mask, queries, preferred_element_type=jnp.float32
    )
    key_block_sums = jnp.einsum(
        "na,abf->bnf", block_member_mask, keys, preferred_element_type=jnp.float32
    )
    query_block_sums, key_block_sums = (
        lax.psum(query_block_sums.astype(jnp.bfloat16), "ctx").astype(jnp.float32),
        lax.psum(key_block_sums.astype(jnp.bfloat16), "ctx").astype(jnp.float32),
    )
    seg_root = jnp.sqrt(seg_lengths.astype(jnp.float32))[None, :, None]
    landmark_query_rows = (query_block_sums / seg_root).astype(jnp.bfloat16)
    landmark_key_rows = (key_block_sums / seg_root).astype(jnp.bfloat16)
    state_score_matrix = (
        jnp.einsum("fcb,pfb->fcp", landmark_query_rows, keys, preferred_element_type=jnp.float32)
        * score_scale_factor
    )
    state_peak = jnp.max(state_score_matrix, axis=-1)
    state_exponent = jnp.exp(state_score_matrix - state_peak[..., None])
    state_total = jnp.sum(state_exponent, axis=-1)
    state_running_total = jnp.einsum(
        "ogq,qoc->ogc",
        state_exponent.astype(jnp.bfloat16),
        values,
        preferred_element_type=jnp.float32,
    )
    start_state = (
        jnp.full((heads_here, landmarks), very_negative, jnp.float32),
        jnp.zeros((heads_here, landmarks), jnp.float32),
        jnp.zeros((heads_here, landmarks, head_dim), jnp.float32),
    )
    in_peak, in_total, in_acc = prefix(
        (state_peak, state_total, state_running_total), "ctx", merge_states, start_state
    )
    attention_kernel = jax.nn.softmax(
        jnp.einsum(
            "slu,szu->slz",
            landmark_query_rows,
            landmark_key_rows,
            preferred_element_type=jnp.float32,
        )
        * score_scale_factor,
        axis=-1,
    )
    pseudo_inverse_matrix = newton_inverse(attention_kernel)
    causal = jnp.arange(row_count)[:, None] >= jnp.arange(row_count)[None, :]
    local_scores = (
        jnp.einsum("thd,uhd->htu", queries, keys, preferred_element_type=jnp.float32)
        * score_scale_factor
    )
    local_scores = jnp.where(causal[None], local_scores, very_negative)
    local_probs = jax.nn.softmax(local_scores, axis=-1).astype(jnp.bfloat16)
    local_block_output = jnp.einsum(
        "htu,uhd->thd", local_probs, values, preferred_element_type=jnp.float32
    )
    allowed = seg_ends <= block_start
    landmark_value_rows = jnp.where(
        allowed[None, :, None], in_acc / jnp.maximum(in_total, 1.0)[..., None], 0.0
    )
    blended_state = jnp.einsum(
        "bxz,bzl->bxl", pseudo_inverse_matrix, landmark_value_rows, precision=lax.Precision.HIGHEST
    ).astype(jnp.bfloat16)
    landmark_score_matrix = (
        jnp.einsum("byz,yfz->ybf", queries, landmark_key_rows, preferred_element_type=jnp.float32)
        * score_scale_factor
    )
    landmark_weight_matrix = masked_weights(landmark_score_matrix, allowed[None, None, :]).astype(
        jnp.bfloat16
    )
    land_out = jnp.einsum(
        "ecp,epy->cey", landmark_weight_matrix, blended_state, preferred_element_type=jnp.float32
    )
    landmark_attention_layer = (
        (local_block_output + land_out)
        .astype(jnp.bfloat16)
        .reshape(row_count, heads_here * head_dim)
    )
    partial_value = jnp.dot(
        landmark_attention_layer, out_weight, preferred_element_type=jnp.float32
    )
    return lax.psum_scatter(
        partial_value.astype(jnp.bfloat16), "tp", scatter_dimension=1, tiled=True
    )


MESH_ID = pl.DeviceIdType.MESH
HIGHEST = lax.Precision.HIGHEST
NT = (((1,), (1,)), ((), ()))
TN = (((0,), (0,)), ((), ()))


def front_kernel(
    n, q_ref, k_ref, v_ref, len_row_ref, len_col_ref, out_ref,
    sum_out, sum_in, land, acc_out, acc_in, stat_out, stat_in,
    mix_out, mix_in, local, weights, send_sem, recv_sem,
):
    heads, rows, hd = q_ref.shape
    marks = len_row_ref.shape[1]
    scale = hd ** (-0.5)
    me = lax.axis_index("ctx")
    f32, bf16 = jnp.float32, jnp.bfloat16

    def push(phase, src, dst, peer):
        return pltpu.make_async_remote_copy(
            src_ref=src, dst_ref=dst,
            send_sem=send_sem.at[phase, peer], recv_sem=recv_sem.at[phase, me],
            device_id={"ctx": peer}, device_id_type=MESH_ID,
        )

    def arrival(phase, src, dst, peer):
        return pltpu.make_async_remote_copy(
            src_ref=src, dst_ref=dst,
            send_sem=send_sem.at[phase, peer], recv_sem=recv_sem.at[phase, peer],
            device_id={"ctx": peer}, device_id_type=MESH_ID,
        )

    barrier = pltpu.get_barrier_semaphore()
    for o in range(1, n):
        pl.semaphore_signal(
            barrier, inc=1, device_id={"ctx": lax.rem(me + o, n)}, device_id_type=MESH_ID
        )

    low = lax.broadcasted_iota(jnp.int32, (marks, marks), 0)
    high = lax.broadcasted_iota(jnp.int32, (marks, marks), 1)
    len_row = len_row_ref[...].astype(f32)
    len_col = len_col_ref[...].astype(f32)
    ends_col = jnp.sum(jnp.where(high <= low, len_row, 0.0), axis=1, keepdims=True)
    ends_row = jnp.sum(jnp.where(low <= high, len_col, 0.0), axis=0, keepdims=True)
    begins_col = ends_col - len_col
    root_col = jnp.sqrt(len_col)
    position = (
        me * rows + lax.broadcasted_iota(jnp.int32, (marks, rows), 1)
    ).astype(f32)
    member = jnp.where(
        (position >= begins_col) & (position < ends_col), 1.0, 0.0
    ).astype(bf16)

    def block_sums(p):
        return (
            jnp.dot(member, q_ref[p], preferred_element_type=f32).astype(bf16),
            jnp.dot(member, k_ref[p], preferred_element_type=f32).astype(bf16),
        )

    pl.semaphore_wait(barrier, n - 1)

    def send_sums(o, _):
        p = lax.rem(me + o, n)
        sum_out[p, 0], sum_out[p, 1] = block_sums(p)
        push(0, sum_out.at[p], sum_in.at[me], p).start()
        return 0

    lax.fori_loop(1, n, send_sums, 0)
    own_q, own_k = block_sums(me)
    sum_in[me, 0] = own_q
    sum_in[me, 1] = own_k

    half = rows // 2
    low_t = lax.broadcasted_iota(jnp.int32, (half, half), 0)
    low_u = lax.broadcasted_iota(jnp.int32, (half, half), 1)
    diagonal = low_t >= low_u

    def local_head(h, _):
        q, k, v = q_ref[h], k_ref[h], v_ref[h]
        s0 = lax.dot_general(q[:half], k[:half], NT, preferred_element_type=f32) * scale
        s0 = jnp.where(diagonal, s0, very_negative)
        e0 = jnp.exp(s0 - jnp.max(s0, axis=1, keepdims=True))
        n0 = jnp.sum(e0, axis=1, keepdims=True)
        local[h, :half] = jnp.dot(e0.astype(bf16), v[:half], preferred_element_type=f32) / n0
        s1 = lax.dot_general(q[half:], k[:half], NT, preferred_element_type=f32) * scale
        s2 = lax.dot_general(q[half:], k[half:], NT, preferred_element_type=f32) * scale
        s2 = jnp.where(diagonal, s2, very_negative)
        top = jnp.maximum(
            jnp.max(s1, axis=1, keepdims=True), jnp.max(s2, axis=1, keepdims=True)
        )
        e1 = jnp.exp(s1 - top)
        e2 = jnp.exp(s2 - top)
        n1 = jnp.sum(e1, axis=1, keepdims=True) + jnp.sum(e2, axis=1, keepdims=True)
        local[h, half:] = (
            jnp.dot(e1.astype(bf16), v[:half], preferred_element_type=f32)
            + jnp.dot(e2.astype(bf16), v[half:], preferred_element_type=f32)
        ) / n1
        return 0

    lax.fori_loop(0, heads, local_head, 0)

    def wait_sums(o, total):
        p = lax.rem(me + o, n)
        arrival(0, sum_out.at[p], sum_in.at[p], p).wait_recv()
        return (total[0] + sum_in[p, 0].astype(f32), total[1] + sum_in[p, 1].astype(f32))

    q_sum, k_sum = lax.fori_loop(
        1, n, wait_sums, (sum_in[me, 0].astype(f32), sum_in[me, 1].astype(f32))
    )
    land_q = (q_sum / root_col).astype(bf16)
    land_k = (k_sum / root_col).astype(bf16)
    land[me, 0] = land_q
    land[me, 1] = land_k

    def send_land(o, _):
        p = lax.rem(me + o, n)
        push(1, land.at[me], land.at[me], p).start()
        return 0

    lax.fori_loop(1, n, send_land, 0)

    def highest(a, b):
        return jnp.dot(a, b, precision=HIGHEST, preferred_element_type=f32)

    scores = lax.dot_general(land_q, land_k, NT, preferred_element_type=f32) * scale
    expo = jnp.exp(scores - jnp.max(scores, axis=1, keepdims=True))
    kernel = expo / jnp.sum(expo, axis=1, keepdims=True)
    row_sum = jnp.max(jnp.sum(kernel, axis=1, keepdims=True), axis=0, keepdims=True)
    col_sum = jnp.max(jnp.sum(kernel, axis=0, keepdims=True), axis=1, keepdims=True)
    eye = jnp.where(low == high, 1.0, 0.0).astype(f32)

    def newton(_, z):
        kz = highest(kernel, z)
        f = 15.0 * eye - highest(kz, 7.0 * eye - kz)
        f = 13.0 * eye - highest(kz, f)
        return 0.25 * highest(z, f)

    pinv = lax.fori_loop(0, ITERS, newton, kernel.T / (row_sum * col_sum))

    def block_state(p):
        st = lax.dot_general(k_ref[p], land[p, 0], NT, preferred_element_type=f32) * scale
        peak = jnp.max(st, axis=0, keepdims=True)
        e = jnp.exp(st - peak)
        total = jnp.sum(e, axis=0, keepdims=True)
        acc = lax.dot_general(v_ref[p], e.astype(bf16), TN, preferred_element_type=f32)
        line = lax.broadcasted_iota(jnp.int32, (8, marks), 0)
        return acc.astype(bf16), jnp.where(line == 0, peak, total)

    def send_states(o, _):
        p = lax.rem(me + o, n)
        arrival(1, land.at[p], land.at[p], p).wait_recv()
        acc_out[p], stat_out[p] = block_state(p)
        push(2, acc_out.at[p], acc_in.at[me], p).start()
        push(3, stat_out.at[p], stat_in.at[me], p).start()
        return 0

    lax.fori_loop(1, n, send_states, 0)
    own_acc, own_stat = block_state(me)
    acc_in[me] = own_acc
    stat_in[me] = own_stat

    allowed_here = ends_row <= (me * rows).astype(f32)

    def land_head(h, _):
        s = lax.dot_general(q_ref[h], land[h, 1], NT, preferred_element_type=f32) * scale
        s = jnp.where(allowed_here, s, very_negative)
        e = jnp.where(allowed_here, jnp.exp(s - jnp.max(s, axis=1, keepdims=True)), 0.0)
        weights[h] = (e / jnp.maximum(jnp.sum(e, axis=1, keepdims=True), 1.0)).astype(bf16)
        return 0

    lax.fori_loop(0, heads, land_head, 0)

    def scan_block(b, carry):
        peak, total, acc = carry
        allowed = ends_row <= (b * rows).astype(f32)
        lv = jnp.where(allowed, acc / jnp.maximum(total, 1.0), 0.0)
        mixed = lax.dot_general(
            lv, pinv, NT, precision=HIGHEST, preferred_element_type=f32
        ).astype(bf16)

        @pl.when(b == me)
        def _():
            mix_in[me] = mixed

        @pl.when(b != me)
        def _():
            mix_out[b] = mixed
            push(4, mix_out.at[b], mix_in.at[me], b).start()
            arrival(2, acc_out.at[b], acc_in.at[b], b).wait_recv()
            arrival(3, stat_out.at[b], stat_in.at[b], b).wait_recv()

        stat = stat_in[b]
        new_peak, new_total = stat[0:1], stat[1:2]
        top = jnp.maximum(peak, new_peak)
        first = jnp.exp(peak - top)
        second = jnp.exp(new_peak - top)
        return (
            top,
            total * first + new_total * second,
            acc * first + acc_in[b].astype(f32) * second,
        )

    lax.fori_loop(
        0, n, scan_block,
        (
            jnp.full((1, marks), very_negative, f32),
            jnp.zeros((1, marks), f32),
            jnp.zeros((hd, marks), f32),
        ),
    )

    def finish(o, _):
        h = lax.rem(me + o, n)

        @pl.when(h != me)
        def _():
            arrival(4, mix_out.at[h], mix_in.at[h], h).wait_recv()

        land_out = lax.dot_general(weights[h], mix_in[h], NT, preferred_element_type=f32)
        at = pl.multiple_of(h * hd, hd)
        out_ref[:, pl.ds(at, hd)] = (local[h] + land_out).astype(bf16)
        return 0

    lax.fori_loop(0, n, finish, 0)

    def drain(o, _):
        p = lax.rem(me + o, n)
        push(0, sum_out.at[p], sum_in.at[me], p).wait_send()
        push(1, land.at[me], land.at[me], p).wait_send()
        push(2, acc_out.at[p], acc_in.at[me], p).wait_send()
        push(3, stat_out.at[p], stat_in.at[me], p).wait_send()
        push(4, mix_out.at[p], mix_in.at[me], p).wait_send()
        return 0

    lax.fori_loop(1, n, drain, 0)


def front(queries, keys, values, seg_lengths):
    rows, heads, hd = queries.shape
    n = lax.axis_size("ctx")
    marks = seg_lengths.shape[0]
    by_head = lambda x: jnp.swapaxes(x, 0, 1)
    bf16, f32 = jnp.bfloat16, jnp.float32
    return pl.pallas_call(
        functools.partial(front_kernel, n),
        out_shape=jax.ShapeDtypeStruct((rows, heads * hd), bf16),
        in_specs=[pl.BlockSpec(memory_space=pltpu.VMEM)] * 5,
        out_specs=pl.BlockSpec(memory_space=pltpu.VMEM),
        scratch_shapes=[
            pltpu.VMEM((n, 2, marks, hd), bf16),
            pltpu.VMEM((n, 2, marks, hd), bf16),
            pltpu.VMEM((n, 2, marks, hd), bf16),
            pltpu.VMEM((n, hd, marks), bf16),
            pltpu.VMEM((n, hd, marks), bf16),
            pltpu.VMEM((n, 8, marks), f32),
            pltpu.VMEM((n, 8, marks), f32),
            pltpu.VMEM((n, hd, marks), bf16),
            pltpu.VMEM((n, hd, marks), bf16),
            pltpu.VMEM((heads, rows, hd), f32),
            pltpu.VMEM((heads, rows, marks), bf16),
            pltpu.SemaphoreType.DMA((5, n)),
            pltpu.SemaphoreType.DMA((5, n)),
        ],
        compiler_params=pltpu.CompilerParams(
            collective_id=0, has_side_effects=True, vmem_limit_bytes=40 << 20
        ),
        name="front",
    )(
        by_head(queries), by_head(keys), by_head(values),
        seg_lengths[None, :], seg_lengths[:, None],
    )


def on_device_by_head(queries, keys, values, seg_lengths, out_weight):
    attention = front(queries, keys, values, seg_lengths)
    partial_value = jnp.dot(attention, out_weight, preferred_element_type=jnp.float32)
    return lax.psum_scatter(
        partial_value.astype(jnp.bfloat16), "tp", scatter_dimension=1, tiled=True
    )


def on_device_any(queries, keys, values, seg_lengths, out_weight):
    one_head_each = queries.shape[1] == lax.axis_size("ctx")
    body = on_device_by_head if one_head_each else on_device
    return body(queries, keys, values, seg_lengths, out_weight)


def solution(mesh):
    in_specs = (
        P("ctx", "tp", None),
        P("ctx", "tp", None),
        P("ctx", "tp", None),
        P(),
        P("tp", None),
    )
    out_specs = P("ctx", "tp")
    return jax.shard_map(
        on_device_any, mesh=mesh, in_specs=in_specs, out_specs=out_specs, check_vma=False
    )
```

```python
import functools

import jax
import jax.numpy as jnp
from jax import lax
from jax.experimental import pallas as pl
from jax.experimental.pallas import tpu as pltpu
from jax.sharding import PartitionSpec as P

ITERS = 6


very_negative = -1e30


def prefix(shard, axis, combine, identity):
    peers, index = (lax.axis_size(axis), lax.axis_index(axis))
    everything = jax.tree.map(
        lambda part, kind: lax.all_gather(part.astype(kind), axis),
        shard,
        (jnp.bfloat16, jnp.bfloat16, jnp.bfloat16),
    )
    start = jax.tree.map(
        lambda part, zero: jnp.broadcast_to(jnp.asarray(zero, part.dtype), part.shape),
        shard,
        identity,
    )

    def lap(k, before):
        reached = k < index
        new = combine(
            before, jax.tree.map(lambda part, own: part[k].astype(own.dtype), everything, shard)
        )
        return jax.tree.map(lambda a, b: jnp.where(reached, a, b), new, before)

    return lax.fori_loop(0, peers, lap, start)


def merge_states(earlier, latter):
    top_peak = jnp.maximum(earlier[0], latter[0])
    first_factor = jnp.exp(earlier[0] - top_peak)
    second_factor = jnp.exp(latter[0] - top_peak)
    return (
        top_peak,
        earlier[1] * first_factor + latter[1] * second_factor,
        earlier[2] * first_factor[..., None] + latter[2] * second_factor[..., None],
    )


def masked_weights(scores, allowed):
    masked = jnp.where(allowed, scores, very_negative)
    top_score = jnp.max(masked, axis=-1, keepdims=True)
    expo = jnp.where(allowed, jnp.exp(masked - top_score), 0.0)
    return expo / jnp.maximum(jnp.sum(expo, axis=-1, keepdims=True), 1.0)


def newton_inverse(attention_kernel):
    highest = lax.Precision.HIGHEST
    row_sum = jnp.max(jnp.sum(attention_kernel, axis=2), axis=-1)
    col_sum = jnp.max(jnp.sum(attention_kernel, axis=1), axis=-1)
    approx = jnp.swapaxes(attention_kernel, 1, 2) / (row_sum * col_sum)[:, None, None]
    identity = jnp.eye(attention_kernel.shape[-1], dtype=jnp.float32)
    for iteration in range(ITERS):
        applied = jnp.einsum("hij,hjk->hik", attention_kernel, approx, precision=highest)
        factor = 7.0 * identity - applied
        factor = 15.0 * identity - jnp.einsum("hij,hjk->hik", applied, factor, precision=highest)
        factor = 13.0 * identity - jnp.einsum("hij,hjk->hik", applied, factor, precision=highest)
        approx = 0.25 * jnp.einsum("hij,hjk->hik", approx, factor, precision=highest)
    return approx


def on_device(queries, keys, values, seg_lengths, out_weight):
    row_count, heads_here, head_dim = queries.shape
    landmarks = seg_lengths.shape[0]
    score_scale_factor = head_dim ** (-0.5)
    block_start = lax.axis_index("ctx") * row_count
    seg_ends = jnp.cumsum(seg_lengths)
    seg_begins = seg_ends - seg_lengths
    position = block_start + jnp.arange(row_count, dtype=jnp.int32)
    block_member_mask = (
        (position[None, :] >= seg_begins[:, None]) & (position[None, :] < seg_ends[:, None])
    ).astype(jnp.bfloat16)
    query_block_sums = jnp.einsum(
        "na,abf->bnf", block_member_mask, queries, preferred_element_type=jnp.float32
    )
    key_block_sums = jnp.einsum(
        "na,abf->bnf", block_member_mask, keys, preferred_element_type=jnp.float32
    )
    query_block_sums, key_block_sums = (
        lax.psum(query_block_sums.astype(jnp.bfloat16), "ctx").astype(jnp.float32),
        lax.psum(key_block_sums.astype(jnp.bfloat16), "ctx").astype(jnp.float32),
    )
    seg_root = jnp.sqrt(seg_lengths.astype(jnp.float32))[None, :, None]
    landmark_query_rows = (query_block_sums / seg_root).astype(jnp.bfloat16)
    landmark_key_rows = (key_block_sums / seg_root).astype(jnp.bfloat16)
    state_score_matrix = (
        jnp.einsum("fcb,pfb->fcp", landmark_query_rows, keys, preferred_element_type=jnp.float32)
        * score_scale_factor
    )
    state_peak = jnp.max(state_score_matrix, axis=-1)
    state_exponent = jnp.exp(state_score_matrix - state_peak[..., None])
    state_total = jnp.sum(state_exponent, axis=-1)
    state_running_total = jnp.einsum(
        "ogq,qoc->ogc",
        state_exponent.astype(jnp.bfloat16),
        values,
        preferred_element_type=jnp.float32,
    )
    start_state = (
        jnp.full((heads_here, landmarks), very_negative, jnp.float32),
        jnp.zeros((heads_here, landmarks), jnp.float32),
        jnp.zeros((heads_here, landmarks, head_dim), jnp.float32),
    )
    in_peak, in_total, in_acc = prefix(
        (state_peak, state_total, state_running_total), "ctx", merge_states, start_state
    )
    attention_kernel = jax.nn.softmax(
        jnp.einsum(
            "slu,szu->slz",
            landmark_query_rows,
            landmark_key_rows,
            preferred_element_type=jnp.float32,
        )
        * score_scale_factor,
        axis=-1,
    )
    pseudo_inverse_matrix = newton_inverse(attention_kernel)
    causal = jnp.arange(row_count)[:, None] >= jnp.arange(row_count)[None, :]
    local_scores = (
        jnp.einsum("thd,uhd->htu", queries, keys, preferred_element_type=jnp.float32)
        * score_scale_factor
    )
    local_scores = jnp.where(causal[None], local_scores, very_negative)
    local_probs = jax.nn.softmax(local_scores, axis=-1).astype(jnp.bfloat16)
    local_block_output = jnp.einsum(
        "htu,uhd->thd", local_probs, values, preferred_element_type=jnp.float32
    )
    allowed = seg_ends <= block_start
    landmark_value_rows = jnp.where(
        allowed[None, :, None], in_acc / jnp.maximum(in_total, 1.0)[..., None], 0.0
    )
    blended_state = jnp.einsum(
        "bxz,bzl->bxl", pseudo_inverse_matrix, landmark_value_rows, precision=lax.Precision.HIGHEST
    ).astype(jnp.bfloat16)
    landmark_score_matrix = (
        jnp.einsum("byz,yfz->ybf", queries, landmark_key_rows, preferred_element_type=jnp.float32)
        * score_scale_factor
    )
    landmark_weight_matrix = masked_weights(landmark_score_matrix, allowed[None, None, :]).astype(
        jnp.bfloat16
    )
    land_out = jnp.einsum(
        "ecp,epy->cey", landmark_weight_matrix, blended_state, preferred_element_type=jnp.float32
    )
    landmark_attention_layer = (
        (local_block_output + land_out)
        .astype(jnp.bfloat16)
        .reshape(row_count, heads_here * head_dim)
    )
    partial_value = jnp.dot(
        landmark_attention_layer, out_weight, preferred_element_type=jnp.float32
    )
    return lax.psum_scatter(
        partial_value.astype(jnp.bfloat16), "tp", scatter_dimension=1, tiled=True
    )


MESH_ID = pl.DeviceIdType.MESH
HIGHEST = lax.Precision.HIGHEST
CHUNKS = 4
NT = (((1,), (1,)), ((), ()))
TN = (((0,), (0,)), ((), ()))


def layer_kernel(
    n, q_ref, k_ref, v_ref, len_row_ref, len_col_ref, w_hbm, out_ref,
    sum_out, sum_in, land, acc_out, acc_in, stat_out, stat_in,
    mix_out, mix_in, local, weights, att, w_own, w_outer,
    far_out, near_out, cross_out, own_out, outer_in, att_in, far_in, cross_in,
    send_sem, recv_sem, load_sem, wsend_sem, wrecv_sem, zsend_sem, zrecv_sem,
):
    heads, rows, hd = q_ref.shape
    marks = len_row_ref.shape[1]
    scale = hd ** (-0.5)
    me = lax.axis_index("ctx")
    f32, bf16 = jnp.float32, jnp.bfloat16

    def push(phase, src, dst, peer):
        return pltpu.make_async_remote_copy(
            src_ref=src, dst_ref=dst,
            send_sem=send_sem.at[phase, peer], recv_sem=recv_sem.at[phase, me],
            device_id={"ctx": peer}, device_id_type=MESH_ID,
        )

    def arrival(phase, src, dst, peer):
        return pltpu.make_async_remote_copy(
            src_ref=src, dst_ref=dst,
            send_sem=send_sem.at[phase, peer], recv_sem=recv_sem.at[phase, peer],
            device_id={"ctx": peer}, device_id_type=MESH_ID,
        )

    t = lax.axis_index("tp")
    side = t // 2
    near_end, far_end = 3 * side, 3 - 3 * side
    mid, cross = 1 + side, 2 - side
    is_end = (t == near_end)
    is_mid = (t == mid)
    cols = out_ref.shape[1]
    chunk = rows // CHUNKS

    loads = [
        pltpu.make_async_copy(
            w_hbm.at[:, pl.ds(j * cols, cols)], w_own.at[j], load_sem.at[j]
        )
        for j in range(4)
    ]
    for load in loads:
        load.start()

    core = lax.rem(me, 2)
    sibling = me + 1 - 2 * core
    part = w_hbm.shape[0] // 2
    part_rows = pl.ds(pl.multiple_of(core * part, part), part)
    other_rows = pl.ds(pl.multiple_of(part - core * part, part), part)

    def weight_hop(i, column):
        return pltpu.make_async_remote_copy(
            src_ref=w_hbm.at[part_rows, pl.ds(pl.multiple_of(column * cols, cols), cols)],
            dst_ref=w_outer.at[i, part_rows],
            send_sem=wsend_sem.at[i], recv_sem=wrecv_sem.at[i],
            device_id={"tp": mid}, device_id_type=MESH_ID,
        )

    def weight_share(i, which):
        return pltpu.make_async_remote_copy(
            src_ref=w_outer.at[i, which], dst_ref=w_outer.at[i, which],
            send_sem=wsend_sem.at[2 + i], recv_sem=wrecv_sem.at[2 + i],
            device_id={"ctx": sibling}, device_id_type=MESH_ID,
        )

    def line_copy(kind, c, src, dst, to):
        at = pl.ds(c * chunk, chunk)
        return pltpu.make_async_remote_copy(
            src_ref=src.at[at], dst_ref=dst.at[at],
            send_sem=zsend_sem.at[kind, c], recv_sem=zrecv_sem.at[kind, c],
            device_id={"tp": to}, device_id_type=MESH_ID,
        )

    def project(dst, first, count, src, w, j, add=None):
        step = 256
        here = pl.ds(first, count)

        def tile(i, _):
            at = pl.ds(pl.multiple_of(i * step, step), step)
            y = jnp.dot(src[here], w[j, :, at], preferred_element_type=f32)
            if add is not None:
                y = y + add[here, at].astype(f32)
            dst[here, at] = y.astype(bf16)
            return 0

        lax.fori_loop(0, cols // step, tile, 0)

    barrier = pltpu.get_barrier_semaphore()

    @pl.when(is_end)
    def _():
        pl.semaphore_signal(barrier, inc=1, device_id={"tp": mid}, device_id_type=MESH_ID)

    @pl.when(is_mid)
    def _():
        pl.semaphore_signal(barrier, inc=1, device_id={"tp": near_end}, device_id_type=MESH_ID)
        pl.semaphore_signal(barrier, inc=1, device_id={"tp": cross}, device_id_type=MESH_ID)

    for o in range(1, n):
        pl.semaphore_signal(
            barrier, inc=1, device_id={"ctx": lax.rem(me + o, n)}, device_id_type=MESH_ID
        )

    low = lax.broadcasted_iota(jnp.int32, (marks, marks), 0)
    high = lax.broadcasted_iota(jnp.int32, (marks, marks), 1)
    len_row = len_row_ref[...].astype(f32)
    len_col = len_col_ref[...].astype(f32)
    ends_col = jnp.sum(jnp.where(high <= low, len_row, 0.0), axis=1, keepdims=True)
    ends_row = jnp.sum(jnp.where(low <= high, len_col, 0.0), axis=0, keepdims=True)
    begins_col = ends_col - len_col
    root_col = jnp.sqrt(len_col)
    position = (
        me * rows + lax.broadcasted_iota(jnp.int32, (marks, rows), 1)
    ).astype(f32)
    member = jnp.where(
        (position >= begins_col) & (position < ends_col), 1.0, 0.0
    ).astype(bf16)

    def block_sums(p):
        return (
            jnp.dot(member, q_ref[p], preferred_element_type=f32).astype(bf16),
            jnp.dot(member, k_ref[p], preferred_element_type=f32).astype(bf16),
        )

    @pl.when(is_end)
    def _():
        pl.semaphore_wait(barrier, n)

    @pl.when(is_mid)
    def _():
        pl.semaphore_wait(barrier, n + 1)

    @pl.when(is_end)
    def _():
        weight_hop(0, mid).start()
        weight_hop(1, cross).start()

    def send_sums(o, _):
        p = lax.rem(me + o, n)
        sum_out[p, 0], sum_out[p, 1] = block_sums(p)
        push(0, sum_out.at[p], sum_in.at[me], p).start()
        return 0

    lax.fori_loop(1, n, send_sums, 0)
    own_q, own_k = block_sums(me)
    sum_in[me, 0] = own_q
    sum_in[me, 1] = own_k

    half = rows // 2
    low_t = lax.broadcasted_iota(jnp.int32, (half, half), 0)
    low_u = lax.broadcasted_iota(jnp.int32, (half, half), 1)
    diagonal = low_t >= low_u

    def local_head(h, _):
        q, k, v = q_ref[h], k_ref[h], v_ref[h]
        s0 = lax.dot_general(q[:half], k[:half], NT, preferred_element_type=f32) * scale
        s0 = jnp.where(diagonal, s0, very_negative)
        e0 = jnp.exp(s0 - jnp.max(s0, axis=1, keepdims=True))
        n0 = jnp.sum(e0, axis=1, keepdims=True)
        local[h, :half] = jnp.dot(e0.astype(bf16), v[:half], preferred_element_type=f32) / n0
        s1 = lax.dot_general(q[half:], k[:half], NT, preferred_element_type=f32) * scale
        s2 = lax.dot_general(q[half:], k[half:], NT, preferred_element_type=f32) * scale
        s2 = jnp.where(diagonal, s2, very_negative)
        top = jnp.maximum(
            jnp.max(s1, axis=1, keepdims=True), jnp.max(s2, axis=1, keepdims=True)
        )
        e1 = jnp.exp(s1 - top)
        e2 = jnp.exp(s2 - top)
        n1 = jnp.sum(e1, axis=1, keepdims=True) + jnp.sum(e2, axis=1, keepdims=True)
        local[h, half:] = (
            jnp.dot(e1.astype(bf16), v[:half], preferred_element_type=f32)
            + jnp.dot(e2.astype(bf16), v[half:], preferred_element_type=f32)
        ) / n1
        return 0

    lax.fori_loop(0, heads, local_head, 0)

    def wait_sums(o, total):
        p = lax.rem(me + o, n)
        arrival(0, sum_out.at[p], sum_in.at[p], p).wait_recv()
        return (total[0] + sum_in[p, 0].astype(f32), total[1] + sum_in[p, 1].astype(f32))

    q_sum, k_sum = lax.fori_loop(
        1, n, wait_sums, (sum_in[me, 0].astype(f32), sum_in[me, 1].astype(f32))
    )
    land_q = (q_sum / root_col).astype(bf16)
    land_k = (k_sum / root_col).astype(bf16)
    land[me, 0] = land_q
    land[me, 1] = land_k

    def send_land(o, _):
        p = lax.rem(me + o, n)
        push(1, land.at[me], land.at[me], p).start()
        return 0

    lax.fori_loop(1, n, send_land, 0)

    def highest(a, b):
        return jnp.dot(a, b, precision=HIGHEST, preferred_element_type=f32)

    scores = lax.dot_general(land_q, land_k, NT, preferred_element_type=f32) * scale
    expo = jnp.exp(scores - jnp.max(scores, axis=1, keepdims=True))
    kernel = expo / jnp.sum(expo, axis=1, keepdims=True)
    row_sum = jnp.max(jnp.sum(kernel, axis=1, keepdims=True), axis=0, keepdims=True)
    col_sum = jnp.max(jnp.sum(kernel, axis=0, keepdims=True), axis=1, keepdims=True)
    eye = jnp.where(low == high, 1.0, 0.0).astype(f32)

    def newton(_, z):
        kz = highest(kernel, z)
        f = 15.0 * eye - highest(kz, 7.0 * eye - kz)
        f = 13.0 * eye - highest(kz, f)
        return 0.25 * highest(z, f)

    pinv = lax.fori_loop(0, ITERS, newton, kernel.T / (row_sum * col_sum))

    def block_state(p):
        st = lax.dot_general(k_ref[p], land[p, 0], NT, preferred_element_type=f32) * scale
        peak = jnp.max(st, axis=0, keepdims=True)
        e = jnp.exp(st - peak)
        total = jnp.sum(e, axis=0, keepdims=True)
        acc = lax.dot_general(v_ref[p], e.astype(bf16), TN, preferred_element_type=f32)
        line = lax.broadcasted_iota(jnp.int32, (8, marks), 0)
        return acc.astype(bf16), jnp.where(line == 0, peak, total)

    def send_states(o, _):
        p = lax.rem(me + o, n)
        arrival(1, land.at[p], land.at[p], p).wait_recv()
        acc_out[p], stat_out[p] = block_state(p)
        push(2, acc_out.at[p], acc_in.at[me], p).start()
        push(3, stat_out.at[p], stat_in.at[me], p).start()
        return 0

    lax.fori_loop(1, n, send_states, 0)
    own_acc, own_stat = block_state(me)
    acc_in[me] = own_acc
    stat_in[me] = own_stat

    allowed_here = ends_row <= (me * rows).astype(f32)

    def land_head(h, _):
        s = lax.dot_general(q_ref[h], land[h, 1], NT, preferred_element_type=f32) * scale
        s = jnp.where(allowed_here, s, very_negative)
        e = jnp.where(allowed_here, jnp.exp(s - jnp.max(s, axis=1, keepdims=True)), 0.0)
        weights[h] = (e / jnp.maximum(jnp.sum(e, axis=1, keepdims=True), 1.0)).astype(bf16)
        return 0

    lax.fori_loop(0, heads, land_head, 0)

    def scan_block(b, carry):
        peak, total, acc = carry
        allowed = ends_row <= (b * rows).astype(f32)
        lv = jnp.where(allowed, acc / jnp.maximum(total, 1.0), 0.0)
        mixed = lax.dot_general(
            lv, pinv, NT, precision=HIGHEST, preferred_element_type=f32
        ).astype(bf16)

        @pl.when(b == me)
        def _():
            mix_in[me] = mixed

        @pl.when(b != me)
        def _():
            mix_out[b] = mixed
            push(4, mix_out.at[b], mix_in.at[me], b).start()
            arrival(2, acc_out.at[b], acc_in.at[b], b).wait_recv()
            arrival(3, stat_out.at[b], stat_in.at[b], b).wait_recv()

        stat = stat_in[b]
        new_peak, new_total = stat[0:1], stat[1:2]
        top = jnp.maximum(peak, new_peak)
        first = jnp.exp(peak - top)
        second = jnp.exp(new_peak - top)
        return (
            top,
            total * first + new_total * second,
            acc * first + acc_in[b].astype(f32) * second,
        )

    lax.fori_loop(
        0, n, scan_block,
        (
            jnp.full((1, marks), very_negative, f32),
            jnp.zeros((1, marks), f32),
            jnp.zeros((hd, marks), f32),
        ),
    )

    def finish(o, _):
        h = lax.rem(me + o, n)

        @pl.when(h != me)
        def _():
            arrival(4, mix_out.at[h], mix_in.at[h], h).wait_recv()

        land_out = lax.dot_general(weights[h], mix_in[h], NT, preferred_element_type=f32)
        at = pl.multiple_of(h * hd, hd)
        att[:, pl.ds(at, hd)] = (local[h] + land_out).astype(bf16)
        return 0

    lax.fori_loop(0, n, finish, 0)
    for load in loads:
        load.wait()

    @pl.when(is_end)
    def _():
        for c in range(CHUNKS):
            project(far_out, c * chunk, chunk, att, w_own, far_end)
            if c >= 2:
                line_copy(0, c - 2, far_out, outer_in, mid).wait_send()
            line_copy(0, c, far_out, outer_in, mid).start()
        project(own_out, 0, rows, att, w_own, t)
        for c in range(CHUNKS):
            if c < 2:
                line_copy(0, CHUNKS - 2 + c, far_out, outer_in, mid).wait_send()
            else:
                line_copy(1, c - 2, att, att_in, mid).wait_send()
            line_copy(1, c, att, att_in, mid).start()
        for c in range(CHUNKS):
            at = pl.ds(c * chunk, chunk)
            line_copy(4, c, near_out, outer_in, mid).wait_recv()
            out_ref[at] = (own_out[at].astype(f32) + outer_in[at].astype(f32)).astype(bf16)
        for c in range(CHUNKS - 2, CHUNKS):
            line_copy(1, c, att, att_in, mid).wait_send()
        weight_hop(0, mid).wait_send()
        weight_hop(1, cross).wait_send()

    @pl.when(is_mid)
    def _():
        project(far_out, 0, rows, att, w_own, far_end)
        for i in range(2):
            weight_hop(i, mid).wait_recv()
            weight_share(i, part_rows).start()
        project(near_out, 0, rows, att, w_own, near_end)
        project(cross_out, 0, rows, att, w_own, cross)
        project(own_out, 0, rows, att, w_own, t)

        def pass_near(c):
            at = pl.ds(c * chunk, chunk)
            line_copy(2, c, far_out, far_in, cross).wait_recv()
            near_out[at] = (near_out[at].astype(f32) + far_in[at].astype(f32)).astype(bf16)
            line_copy(4, c, near_out, outer_in, near_end).start()

        for c in range(CHUNKS):
            at = pl.ds(c * chunk, chunk)
            line_copy(0, c, far_out, outer_in, near_end).wait_recv()
            far_out[at] = (far_out[at].astype(f32) + outer_in[at].astype(f32)).astype(bf16)
            line_copy(2, c, far_out, far_in, cross).start()
            if c >= 1:
                pass_near(c - 1)
        for i in range(2):
            weight_share(i, other_rows).wait_recv()
        for c in range(CHUNKS):
            line_copy(1, c, att, att_in, near_end).wait_recv()
            project(cross_out, c * chunk, chunk, att_in, w_outer, 1, cross_out)
            line_copy(3, c, cross_out, cross_in, cross).start()
            project(own_out, c * chunk, chunk, att_in, w_outer, 0, own_out)
            if c == 0:
                pass_near(CHUNKS - 1)
        for c in range(CHUNKS):
            at = pl.ds(c * chunk, chunk)
            line_copy(3, c, cross_out, cross_in, cross).wait_recv()
            out_ref[at] = (own_out[at].astype(f32) + cross_in[at].astype(f32)).astype(bf16)
        for i in range(2):
            weight_share(i, part_rows).wait_send()
        for c in range(CHUNKS):
            line_copy(2, c, far_out, far_in, cross).wait_send()
            line_copy(3, c, cross_out, cross_in, cross).wait_send()
            line_copy(4, c, near_out, outer_in, near_end).wait_send()

    def drain(o, _):
        p = lax.rem(me + o, n)
        push(0, sum_out.at[p], sum_in.at[me], p).wait_send()
        push(1, land.at[me], land.at[me], p).wait_send()
        push(2, acc_out.at[p], acc_in.at[me], p).wait_send()
        push(3, stat_out.at[p], stat_in.at[me], p).wait_send()
        push(4, mix_out.at[p], mix_in.at[me], p).wait_send()
        return 0

    lax.fori_loop(1, n, drain, 0)


def layer(queries, keys, values, seg_lengths, out_weight):
    rows, heads, hd = queries.shape
    n = lax.axis_size("ctx")
    marks = seg_lengths.shape[0]
    depth = out_weight.shape[0]
    cols = out_weight.shape[1] // 4
    by_head = lambda x: jnp.swapaxes(x, 0, 1)
    bf16, f32 = jnp.bfloat16, jnp.float32
    return pl.pallas_call(
        functools.partial(layer_kernel, n),
        out_shape=jax.ShapeDtypeStruct((rows, cols), bf16),
        in_specs=[pl.BlockSpec(memory_space=pltpu.VMEM)] * 5
        + [pl.BlockSpec(memory_space=pl.ANY)],
        out_specs=pl.BlockSpec(memory_space=pltpu.VMEM),
        scratch_shapes=[
            pltpu.VMEM((n, 2, marks, hd), bf16),
            pltpu.VMEM((n, 2, marks, hd), bf16),
            pltpu.VMEM((n, 2, marks, hd), bf16),
            pltpu.VMEM((n, hd, marks), bf16),
            pltpu.VMEM((n, hd, marks), bf16),
            pltpu.VMEM((n, 8, marks), f32),
            pltpu.VMEM((n, 8, marks), f32),
            pltpu.VMEM((n, hd, marks), bf16),
            pltpu.VMEM((n, hd, marks), bf16),
            pltpu.VMEM((heads, rows, hd), f32),
            pltpu.VMEM((heads, rows, marks), bf16),
            pltpu.VMEM((rows, depth), bf16),
            pltpu.VMEM((4, depth, cols), bf16),
            pltpu.VMEM((2, depth, cols), bf16),
            pltpu.VMEM((rows, cols), bf16),
            pltpu.VMEM((rows, cols), bf16),
            pltpu.VMEM((rows, cols), bf16),
            pltpu.VMEM((rows, cols), bf16),
            pltpu.VMEM((rows, cols), bf16),
            pltpu.VMEM((rows, depth), bf16),
            pltpu.VMEM((rows, cols), bf16),
            pltpu.VMEM((rows, cols), bf16),
            pltpu.SemaphoreType.DMA((5, n)),
            pltpu.SemaphoreType.DMA((5, n)),
            pltpu.SemaphoreType.DMA((4,)),
            pltpu.SemaphoreType.DMA((4,)),
            pltpu.SemaphoreType.DMA((4,)),
            pltpu.SemaphoreType.DMA((5, CHUNKS)),
            pltpu.SemaphoreType.DMA((5, CHUNKS)),
        ],
        compiler_params=pltpu.CompilerParams(
            collective_id=0, has_side_effects=True, vmem_limit_bytes=56 << 20
        ),
        name="layer",
    )(
        by_head(queries), by_head(keys), by_head(values),
        seg_lengths[None, :], seg_lengths[:, None], out_weight,
    )


def on_device_any(queries, keys, values, seg_lengths, out_weight):
    one_head_each = queries.shape[1] == lax.axis_size("ctx")
    body = layer if one_head_each and lax.axis_size("tp") == 4 else on_device
    return body(queries, keys, values, seg_lengths, out_weight)


def solution(mesh):
    in_specs = (
        P("ctx", "tp", None),
        P("ctx", "tp", None),
        P("ctx", "tp", None),
        P(),
        P("tp", None),
    )
    out_specs = P("ctx", "tp")
    return jax.shard_map(
        on_device_any, mesh=mesh, in_specs=in_specs, out_specs=out_specs, check_vma=False
    )
```

```python
import functools

import jax
import jax.numpy as jnp
from jax import lax
from jax.experimental import pallas as pl
from jax.experimental.pallas import tpu as pltpu
from jax.sharding import PartitionSpec as P

ITERS = 6


very_negative = -1e30


def prefix(shard, axis, combine, identity):
    peers, index = (lax.axis_size(axis), lax.axis_index(axis))
    everything = jax.tree.map(
        lambda part, kind: lax.all_gather(part.astype(kind), axis),
        shard,
        (jnp.bfloat16, jnp.bfloat16, jnp.bfloat16),
    )
    start = jax.tree.map(
        lambda part, zero: jnp.broadcast_to(jnp.asarray(zero, part.dtype), part.shape),
        shard,
        identity,
    )

    def lap(k, before):
        reached = k < index
        new = combine(
            before, jax.tree.map(lambda part, own: part[k].astype(own.dtype), everything, shard)
        )
        return jax.tree.map(lambda a, b: jnp.where(reached, a, b), new, before)

    return lax.fori_loop(0, peers, lap, start)


def merge_states(earlier, latter):
    top_peak = jnp.maximum(earlier[0], latter[0])
    first_factor = jnp.exp(earlier[0] - top_peak)
    second_factor = jnp.exp(latter[0] - top_peak)
    return (
        top_peak,
        earlier[1] * first_factor + latter[1] * second_factor,
        earlier[2] * first_factor[..., None] + latter[2] * second_factor[..., None],
    )


def masked_weights(scores, allowed):
    masked = jnp.where(allowed, scores, very_negative)
    top_score = jnp.max(masked, axis=-1, keepdims=True)
    expo = jnp.where(allowed, jnp.exp(masked - top_score), 0.0)
    return expo / jnp.maximum(jnp.sum(expo, axis=-1, keepdims=True), 1.0)


def newton_inverse(attention_kernel):
    highest = lax.Precision.HIGHEST
    row_sum = jnp.max(jnp.sum(attention_kernel, axis=2), axis=-1)
    col_sum = jnp.max(jnp.sum(attention_kernel, axis=1), axis=-1)
    approx = jnp.swapaxes(attention_kernel, 1, 2) / (row_sum * col_sum)[:, None, None]
    identity = jnp.eye(attention_kernel.shape[-1], dtype=jnp.float32)
    for iteration in range(ITERS):
        applied = jnp.einsum("hij,hjk->hik", attention_kernel, approx, precision=highest)
        factor = 7.0 * identity - applied
        factor = 15.0 * identity - jnp.einsum("hij,hjk->hik", applied, factor, precision=highest)
        factor = 13.0 * identity - jnp.einsum("hij,hjk->hik", applied, factor, precision=highest)
        approx = 0.25 * jnp.einsum("hij,hjk->hik", approx, factor, precision=highest)
    return approx


def on_device(queries, keys, values, seg_lengths, out_weight):
    row_count, heads_here, head_dim = queries.shape
    landmarks = seg_lengths.shape[0]
    score_scale_factor = head_dim ** (-0.5)
    block_start = lax.axis_index("ctx") * row_count
    seg_ends = jnp.cumsum(seg_lengths)
    seg_begins = seg_ends - seg_lengths
    position = block_start + jnp.arange(row_count, dtype=jnp.int32)
    block_member_mask = (
        (position[None, :] >= seg_begins[:, None]) & (position[None, :] < seg_ends[:, None])
    ).astype(jnp.bfloat16)
    query_block_sums = jnp.einsum(
        "na,abf->bnf", block_member_mask, queries, preferred_element_type=jnp.float32
    )
    key_block_sums = jnp.einsum(
        "na,abf->bnf", block_member_mask, keys, preferred_element_type=jnp.float32
    )
    query_block_sums, key_block_sums = (
        lax.psum(query_block_sums.astype(jnp.bfloat16), "ctx").astype(jnp.float32),
        lax.psum(key_block_sums.astype(jnp.bfloat16), "ctx").astype(jnp.float32),
    )
    seg_root = jnp.sqrt(seg_lengths.astype(jnp.float32))[None, :, None]
    landmark_query_rows = (query_block_sums / seg_root).astype(jnp.bfloat16)
    landmark_key_rows = (key_block_sums / seg_root).astype(jnp.bfloat16)
    state_score_matrix = (
        jnp.einsum("fcb,pfb->fcp", landmark_query_rows, keys, preferred_element_type=jnp.float32)
        * score_scale_factor
    )
    state_peak = jnp.max(state_score_matrix, axis=-1)
    state_exponent = jnp.exp(state_score_matrix - state_peak[..., None])
    state_total = jnp.sum(state_exponent, axis=-1)
    state_running_total = jnp.einsum(
        "ogq,qoc->ogc",
        state_exponent.astype(jnp.bfloat16),
        values,
        preferred_element_type=jnp.float32,
    )
    start_state = (
        jnp.full((heads_here, landmarks), very_negative, jnp.float32),
        jnp.zeros((heads_here, landmarks), jnp.float32),
        jnp.zeros((heads_here, landmarks, head_dim), jnp.float32),
    )
    in_peak, in_total, in_acc = prefix(
        (state_peak, state_total, state_running_total), "ctx", merge_states, start_state
    )
    attention_kernel = jax.nn.softmax(
        jnp.einsum(
            "slu,szu->slz",
            landmark_query_rows,
            landmark_key_rows,
            preferred_element_type=jnp.float32,
        )
        * score_scale_factor,
        axis=-1,
    )
    pseudo_inverse_matrix = newton_inverse(attention_kernel)
    causal = jnp.arange(row_count)[:, None] >= jnp.arange(row_count)[None, :]
    local_scores = (
        jnp.einsum("thd,uhd->htu", queries, keys, preferred_element_type=jnp.float32)
        * score_scale_factor
    )
    local_scores = jnp.where(causal[None], local_scores, very_negative)
    local_probs = jax.nn.softmax(local_scores, axis=-1).astype(jnp.bfloat16)
    local_block_output = jnp.einsum(
        "htu,uhd->thd", local_probs, values, preferred_element_type=jnp.float32
    )
    allowed = seg_ends <= block_start
    landmark_value_rows = jnp.where(
        allowed[None, :, None], in_acc / jnp.maximum(in_total, 1.0)[..., None], 0.0
    )
    blended_state = jnp.einsum(
        "bxz,bzl->bxl", pseudo_inverse_matrix, landmark_value_rows, precision=lax.Precision.HIGHEST
    ).astype(jnp.bfloat16)
    landmark_score_matrix = (
        jnp.einsum("byz,yfz->ybf", queries, landmark_key_rows, preferred_element_type=jnp.float32)
        * score_scale_factor
    )
    landmark_weight_matrix = masked_weights(landmark_score_matrix, allowed[None, None, :]).astype(
        jnp.bfloat16
    )
    land_out = jnp.einsum(
        "ecp,epy->cey", landmark_weight_matrix, blended_state, preferred_element_type=jnp.float32
    )
    landmark_attention_layer = (
        (local_block_output + land_out)
        .astype(jnp.bfloat16)
        .reshape(row_count, heads_here * head_dim)
    )
    partial_value = jnp.dot(
        landmark_attention_layer, out_weight, preferred_element_type=jnp.float32
    )
    return lax.psum_scatter(
        partial_value.astype(jnp.bfloat16), "tp", scatter_dimension=1, tiled=True
    )


MESH_ID = pl.DeviceIdType.MESH
HIGHEST = lax.Precision.HIGHEST
CHUNKS = 8
DEPTH = 3
NT = (((1,), (1,)), ((), ()))
TN = (((0,), (0,)), ((), ()))


def layer_kernel(
    n, q_ref, k_ref, v_ref, len_ref, w_hbm, out_ref,
    sum_out, sum_in, land, acc_out, acc_in, stat_out, stat_in,
    mix_out, mix_in, local, weights, att, w_own, w_outer,
    far_out, near_out, cross_out, own_out, outer_in, att_in, far_in, cross_in,
    send_sem, recv_sem, load_sem, wsend_sem, wrecv_sem, zsend_sem, zrecv_sem,
):
    heads, rows, hd = q_ref.shape
    marks = len_ref.shape[1]
    scale = hd ** (-0.5)
    me = lax.axis_index("ctx")
    f32, bf16 = jnp.float32, jnp.bfloat16

    def push(phase, src, dst, peer):
        return pltpu.make_async_remote_copy(
            src_ref=src, dst_ref=dst,
            send_sem=send_sem.at[phase, peer], recv_sem=recv_sem.at[phase, me],
            device_id={"ctx": peer}, device_id_type=MESH_ID,
        )

    def arrival(phase, src, dst, peer):
        return pltpu.make_async_remote_copy(
            src_ref=src, dst_ref=dst,
            send_sem=send_sem.at[phase, peer], recv_sem=recv_sem.at[phase, peer],
            device_id={"ctx": peer}, device_id_type=MESH_ID,
        )

    t = lax.axis_index("tp")
    side = t // 2
    near_end, far_end = 3 * side, 3 - 3 * side
    mid, cross = 1 + side, 2 - side
    is_end = (t == near_end)
    is_mid = (t == mid)
    cols = out_ref.shape[1]
    chunk = rows // CHUNKS

    loads = [
        pltpu.make_async_copy(
            w_hbm.at[:, pl.ds(j * cols, cols)], w_own.at[j], load_sem.at[j]
        )
        for j in range(4)
    ]
    for load in loads:
        load.start()

    core = lax.rem(me, 2)
    sibling = me + 1 - 2 * core
    part = w_hbm.shape[0] // 4
    axis_bit = (2, 4)

    def flipped(i, p):
        return p + axis_bit[i] - 2 * axis_bit[i] * lax.rem(p // axis_bit[i], 2)

    def quarter(i, p):
        q = 2 * lax.rem(p // axis_bit[i], 2) + lax.rem(p, 2)
        return pl.ds(pl.multiple_of(q * part, part), part)

    def weight_hop(i, column):
        return pltpu.make_async_remote_copy(
            src_ref=w_hbm.at[quarter(i, me), pl.ds(pl.multiple_of(column * cols, cols), cols)],
            dst_ref=w_outer.at[i, quarter(i, me)],
            send_sem=wsend_sem.at[i], recv_sem=wrecv_sem.at[i],
            device_id={"tp": mid}, device_id_type=MESH_ID,
        )

    def weight_share(i, step, owner, to):
        return pltpu.make_async_remote_copy(
            src_ref=w_outer.at[i, quarter(i, owner)], dst_ref=w_outer.at[i, quarter(i, owner)],
            send_sem=wsend_sem.at[2 * step + i], recv_sem=wrecv_sem.at[2 * step + i],
            device_id={"ctx": to}, device_id_type=MESH_ID,
        )

    def line_copy(kind, c, src, dst, to):
        at = pl.ds(c * chunk, chunk)
        return pltpu.make_async_remote_copy(
            src_ref=src.at[at], dst_ref=dst.at[at],
            send_sem=zsend_sem.at[kind, c], recv_sem=zrecv_sem.at[kind, c],
            device_id={"tp": to}, device_id_type=MESH_ID,
        )

    def project(dst, first, count, src, w, j, add=None):
        step = 256
        here = pl.ds(first, count)

        def tile(i, _):
            at = pl.ds(pl.multiple_of(i * step, step), step)
            y = jnp.dot(src[here], w[j, :, at], preferred_element_type=f32)
            if add is not None:
                y = y + add[here, at].astype(f32)
            dst[here, at] = y.astype(bf16)
            return 0

        lax.fori_loop(0, cols // step, tile, 0)

    barrier = pltpu.get_barrier_semaphore()

    @pl.when(is_end)
    def _():
        pl.semaphore_signal(barrier, inc=1, device_id={"tp": mid}, device_id_type=MESH_ID)

    @pl.when(is_mid)
    def _():
        pl.semaphore_signal(barrier, inc=1, device_id={"tp": near_end}, device_id_type=MESH_ID)
        pl.semaphore_signal(barrier, inc=1, device_id={"tp": cross}, device_id_type=MESH_ID)

    for o in range(1, n):
        pl.semaphore_signal(
            barrier, inc=1, device_id={"ctx": lax.rem(me + o, n)}, device_id_type=MESH_ID
        )

    low = lax.broadcasted_iota(jnp.int32, (marks, marks), 0)
    high = lax.broadcasted_iota(jnp.int32, (marks, marks), 1)
    len_row = len_ref[...].astype(f32)
    len_col = jnp.broadcast_to(len_row, (8, marks)).T[:, 0:1]
    ends_col = jnp.sum(jnp.where(high <= low, len_row, 0.0), axis=1, keepdims=True)
    ends_row = jnp.sum(jnp.where(low <= high, len_col, 0.0), axis=0, keepdims=True)
    begins_col = ends_col - len_col
    root_col = jnp.sqrt(len_col)
    position = (
        me * rows + lax.broadcasted_iota(jnp.int32, (marks, rows), 1)
    ).astype(f32)
    member = jnp.where(
        (position >= begins_col) & (position < ends_col), 1.0, 0.0
    ).astype(bf16)

    def block_sums(p):
        return (
            jnp.dot(member, q_ref[p], preferred_element_type=f32).astype(bf16),
            jnp.dot(member, k_ref[p], preferred_element_type=f32).astype(bf16),
        )

    @pl.when(is_end)
    def _():
        pl.semaphore_wait(barrier, n)

    @pl.when(is_mid)
    def _():
        pl.semaphore_wait(barrier, n + 1)

    @pl.when(is_end)
    def _():
        weight_hop(0, mid).start()
        weight_hop(1, cross).start()

    def twin(p):
        return p + 1 - 2 * lax.rem(p, 2)

    def hand(phase, src, dst, sent, landed):
        return pltpu.make_async_remote_copy(
            src_ref=src, dst_ref=dst,
            send_sem=send_sem.at[phase, sent], recv_sem=recv_sem.at[phase, landed],
            device_id={"ctx": sibling}, device_id_type=MESH_ID,
        )

    def send_twin(i, _):
        p = twin(lax.rem(me + 2 * i, n))
        sum_out[p, 0], sum_out[p, 1] = block_sums(p)
        hand(0, sum_out.at[p], sum_in.at[p], p, p).start()
        return 0

    def chip_sums(p):
        q_part, k_part = block_sums(p)
        hand(0, sum_out.at[p], sum_in.at[p], p, p).wait_recv()
        return (
            (q_part.astype(f32) + sum_in[p, 0].astype(f32)),
            (k_part.astype(f32) + sum_in[p, 1].astype(f32)),
        )

    def send_sums(i, _):
        p = lax.rem(me + 2 * i, n)
        q_part, k_part = chip_sums(p)
        sum_out[p, 0] = q_part.astype(bf16)
        sum_out[p, 1] = k_part.astype(bf16)
        push(5, sum_out.at[p], sum_in.at[sibling], p).start()
        return 0

    lax.fori_loop(1, n // 2, send_twin, 0)
    send_twin(0, 0)
    lax.fori_loop(1, n // 2, send_sums, 0)
    own_q, own_k = chip_sums(me)
    sum_out[me, 0] = own_q.astype(bf16)
    sum_out[me, 1] = own_k.astype(bf16)

    half = rows // 2
    low_t = lax.broadcasted_iota(jnp.int32, (half, half), 0)
    low_u = lax.broadcasted_iota(jnp.int32, (half, half), 1)
    diagonal = low_t >= low_u

    def local_head(h, _):
        q, k, v = q_ref[h], k_ref[h], v_ref[h]
        s0 = lax.dot_general(q[:half], k[:half], NT, preferred_element_type=f32) * scale
        s0 = jnp.where(diagonal, s0, very_negative)
        e0 = jnp.exp(s0 - jnp.max(s0, axis=1, keepdims=True))
        n0 = jnp.sum(e0, axis=1, keepdims=True)
        local[h, :half] = jnp.dot(e0.astype(bf16), v[:half], preferred_element_type=f32) / n0
        s1 = lax.dot_general(q[half:], k[:half], NT, preferred_element_type=f32) * scale
        s2 = lax.dot_general(q[half:], k[half:], NT, preferred_element_type=f32) * scale
        s2 = jnp.where(diagonal, s2, very_negative)
        top = jnp.maximum(
            jnp.max(s1, axis=1, keepdims=True), jnp.max(s2, axis=1, keepdims=True)
        )
        e1 = jnp.exp(s1 - top)
        e2 = jnp.exp(s2 - top)
        n1 = jnp.sum(e1, axis=1, keepdims=True) + jnp.sum(e2, axis=1, keepdims=True)
        local[h, half:] = (
            jnp.dot(e1.astype(bf16), v[:half], preferred_element_type=f32)
            + jnp.dot(e2.astype(bf16), v[half:], preferred_element_type=f32)
        ) / n1
        return 0

    lax.fori_loop(0, heads, local_head, 0)

    def wait_sums(i, total):
        p = lax.rem(me + 2 * i, n)
        slot = twin(p)
        arrival(5, sum_out.at[p], sum_in.at[slot], p).wait_recv()
        return (total[0] + sum_in[slot, 0].astype(f32), total[1] + sum_in[slot, 1].astype(f32))

    q_sum, k_sum = lax.fori_loop(
        1, n // 2, wait_sums, (sum_out[me, 0].astype(f32), sum_out[me, 1].astype(f32))
    )
    land_q = (q_sum / root_col).astype(bf16)
    land_k = (k_sum / root_col).astype(bf16)
    land[0, me] = land_q
    land[1, me] = land_k

    LAND = (1, 6)

    def land_push(kind, p):
        return push(LAND[kind], land.at[kind, me], land.at[kind, me], p)

    def land_hand(kind, p):
        return hand(LAND[kind], land.at[kind, p], land.at[kind, p], twin(p), p)

    for kind in range(2):
        for i in range(1, n // 2):
            land_push(kind, lax.rem(me + 2 * i, n)).start()
        land_hand(kind, me).start()

    def land_wait(kind, p):
        arrival(LAND[kind], land.at[kind, p], land.at[kind, p], p).wait_recv()

    def highest(a, b):
        return jnp.dot(a, b, precision=HIGHEST, preferred_element_type=f32)

    scores = lax.dot_general(land_q, land_k, NT, preferred_element_type=f32) * scale
    expo = jnp.exp(scores - jnp.max(scores, axis=1, keepdims=True))
    kernel = expo / jnp.sum(expo, axis=1, keepdims=True)
    row_sum = jnp.max(jnp.sum(kernel, axis=1, keepdims=True), axis=0, keepdims=True)
    col_sum = jnp.max(jnp.sum(kernel, axis=0, keepdims=True), axis=1, keepdims=True)
    eye = jnp.where(low == high, 1.0, 0.0).astype(f32)

    def newton(_, z):
        kz = highest(kernel, z)
        f = 15.0 * eye - highest(kz, 7.0 * eye - kz)
        f = 13.0 * eye - highest(kz, f)
        return 0.25 * highest(z, f)

    def block_state(p):
        st = lax.dot_general(k_ref[p], land[0, p], NT, preferred_element_type=f32) * scale
        peak = jnp.max(st, axis=0, keepdims=True)
        e = jnp.exp(st - peak)
        total = jnp.sum(e, axis=0, keepdims=True)
        acc = lax.dot_general(v_ref[p], e.astype(bf16), TN, preferred_element_type=f32)
        line = lax.broadcasted_iota(jnp.int32, (8, marks), 0)
        return acc.astype(bf16), jnp.where(line == 0, peak, total)

    def send_state(p):
        acc_out[p], stat_out[p] = block_state(p)
        push(2, acc_out.at[p], acc_in.at[me], p).start()
        push(3, stat_out.at[p], stat_in.at[me], p).start()

    own_acc, own_stat = block_state(me)
    acc_in[me] = own_acc
    stat_in[me] = own_stat
    early = lax.fori_loop(0, 2, newton, kernel.T / (row_sum * col_sum))

    def relay_q(i, _):
        p = lax.rem(me + 2 * i, n)
        land_wait(0, p)
        land_hand(0, p).start()
        return 0

    lax.fori_loop(1, n // 2, relay_q, 0)

    def near_states(i, _):
        send_state(lax.rem(me + 2 * i, n))
        return 0

    lax.fori_loop(1, n // 2, near_states, 0)

    def relay_k(i, _):
        p = lax.rem(me + 2 * i, n)
        land_wait(1, p)
        land_hand(1, p).start()
        return 0

    lax.fori_loop(1, n // 2, relay_k, 0)

    early = lax.fori_loop(2, 3, newton, early)

    def twin_states(i, _):
        p = twin(lax.rem(me + 2 * i, n))
        land_wait(0, p)
        send_state(p)
        return 0

    lax.fori_loop(1, n // 2, twin_states, 0)
    twin_states(0, 0)
    pinv = lax.fori_loop(3, ITERS, newton, early)

    def wait_k(i, _):
        land_wait(1, twin(lax.rem(me + 2 * i, n)))
        return 0

    lax.fori_loop(0, n // 2, wait_k, 0)

    allowed_here = ends_row <= (me * rows).astype(f32)

    def land_head(h, _):
        s = lax.dot_general(q_ref[h], land[1, h], NT, preferred_element_type=f32) * scale
        s = jnp.where(allowed_here, s, very_negative)
        e = jnp.where(allowed_here, jnp.exp(s - jnp.max(s, axis=1, keepdims=True)), 0.0)
        weights[h] = (e / jnp.maximum(jnp.sum(e, axis=1, keepdims=True), 1.0)).astype(bf16)
        return 0

    lax.fori_loop(0, heads, land_head, 0)

    def scan_block(b, carry):
        peak, total, acc = carry
        allowed = ends_row <= (b * rows).astype(f32)
        lv = jnp.where(allowed, acc / jnp.maximum(total, 1.0), 0.0)
        mixed = lax.dot_general(
            lv, pinv, NT, precision=HIGHEST, preferred_element_type=f32
        ).astype(bf16)

        @pl.when(b == me)
        def _():
            mix_in[me] = mixed

        @pl.when(b != me)
        def _():
            mix_out[b] = mixed
            push(4, mix_out.at[b], mix_in.at[me], b).start()
            arrival(2, acc_out.at[b], acc_in.at[b], b).wait_recv()
            arrival(3, stat_out.at[b], stat_in.at[b], b).wait_recv()

        stat = stat_in[b]
        new_peak, new_total = stat[0:1], stat[1:2]
        top = jnp.maximum(peak, new_peak)
        first = jnp.exp(peak - top)
        second = jnp.exp(new_peak - top)
        return (
            top,
            total * first + new_total * second,
            acc * first + acc_in[b].astype(f32) * second,
        )

    lax.fori_loop(
        0, n, scan_block,
        (
            jnp.full((1, marks), very_negative, f32),
            jnp.zeros((1, marks), f32),
            jnp.zeros((hd, marks), f32),
        ),
    )

    def finish(o, _):
        h = lax.rem(me + o, n)

        @pl.when(h != me)
        def _():
            arrival(4, mix_out.at[h], mix_in.at[h], h).wait_recv()

        land_out = lax.dot_general(weights[h], mix_in[h], NT, preferred_element_type=f32)
        at = pl.multiple_of(h * hd, hd)
        att[:, pl.ds(at, hd)] = (local[h] + land_out).astype(bf16)
        return 0

    lax.fori_loop(0, n, finish, 0)
    for load in loads:
        load.wait()

    @pl.when(is_end)
    def _():
        for c in range(CHUNKS):
            project(far_out, c * chunk, chunk, att, w_own, far_end)
            if c >= DEPTH:
                line_copy(0, c - DEPTH, far_out, outer_in, mid).wait_send()
            line_copy(0, c, far_out, outer_in, mid).start()
        project(own_out, 0, rows, att, w_own, t)
        for c in range(CHUNKS):
            if c < DEPTH:
                line_copy(0, CHUNKS - DEPTH + c, far_out, outer_in, mid).wait_send()
            else:
                line_copy(1, c - DEPTH, att, att_in, mid).wait_send()
            line_copy(1, c, att, att_in, mid).start()
        for c in range(CHUNKS):
            at = pl.ds(c * chunk, chunk)
            line_copy(4, c, near_out, outer_in, mid).wait_recv()
            out_ref[at] = (own_out[at].astype(f32) + outer_in[at].astype(f32)).astype(bf16)
        for c in range(CHUNKS - DEPTH, CHUNKS):
            line_copy(1, c, att, att_in, mid).wait_send()
        weight_hop(0, mid).wait_send()
        weight_hop(1, cross).wait_send()

    @pl.when(is_mid)
    def _():
        project(far_out, 0, rows, att, w_own, far_end)
        for i in range(2):
            weight_hop(i, mid).wait_recv()
            weight_share(i, 1, me, flipped(i, me)).start()
            weight_share(i, 2, me, sibling).start()

        def pass_near(c):
            at = pl.ds(c * chunk, chunk)
            line_copy(2, c, far_out, far_in, cross).wait_recv()
            near_out[at] = (near_out[at].astype(f32) + far_in[at].astype(f32)).astype(bf16)
            line_copy(4, c, near_out, outer_in, near_end).start()

        for c in range(CHUNKS):
            at = pl.ds(c * chunk, chunk)
            line_copy(0, c, far_out, outer_in, near_end).wait_recv()
            far_out[at] = (far_out[at].astype(f32) + outer_in[at].astype(f32)).astype(bf16)
            line_copy(2, c, far_out, far_in, cross).start()
            if c == 0:
                project(near_out, 0, rows, att, w_own, near_end)
            if c == 1:
                project(cross_out, 0, rows, att, w_own, cross)
            if c == 2:
                project(own_out, 0, rows, att, w_own, t)
            if c >= 1:
                pass_near(c - 1)
            if c == CHUNKS // 2:
                for i in range(2):
                    weight_share(i, 1, flipped(i, me), flipped(i, me)).wait_recv()
                    weight_share(i, 3, flipped(i, me), sibling).start()
        for i in range(2):
            weight_share(i, 2, sibling, sibling).wait_recv()
            weight_share(i, 3, flipped(i, sibling), sibling).wait_recv()
        for c in range(CHUNKS):
            line_copy(1, c, att, att_in, near_end).wait_recv()
            project(cross_out, c * chunk, chunk, att_in, w_outer, 1, cross_out)
            line_copy(3, c, cross_out, cross_in, cross).start()
            project(own_out, c * chunk, chunk, att_in, w_outer, 0, own_out)
            if c == 0:
                pass_near(CHUNKS - 1)
        for c in range(CHUNKS):
            at = pl.ds(c * chunk, chunk)
            line_copy(3, c, cross_out, cross_in, cross).wait_recv()
            out_ref[at] = (own_out[at].astype(f32) + cross_in[at].astype(f32)).astype(bf16)
        for i in range(2):
            weight_share(i, 1, me, flipped(i, me)).wait_send()
            weight_share(i, 2, me, sibling).wait_send()
            weight_share(i, 3, flipped(i, me), sibling).wait_send()
        for c in range(CHUNKS):
            line_copy(2, c, far_out, far_in, cross).wait_send()
            line_copy(3, c, cross_out, cross_in, cross).wait_send()
            line_copy(4, c, near_out, outer_in, near_end).wait_send()

    def drain(o, _):
        p = lax.rem(me + o, n)
        push(2, acc_out.at[p], acc_in.at[me], p).wait_send()
        push(3, stat_out.at[p], stat_in.at[me], p).wait_send()
        push(4, mix_out.at[p], mix_in.at[me], p).wait_send()
        return 0

    lax.fori_loop(1, n, drain, 0)

    def drain_pairs(i, _):
        p = lax.rem(me + 2 * i, n)
        push(5, sum_out.at[p], sum_in.at[sibling], p).wait_send()
        for kind in range(2):
            land_push(kind, p).wait_send()
        return 0

    lax.fori_loop(1, n // 2, drain_pairs, 0)

    def drain_hands(i, _):
        p = lax.rem(me + 2 * i, n)
        hand(0, sum_out.at[twin(p)], sum_in.at[twin(p)], twin(p), twin(p)).wait_send()
        for kind in range(2):
            land_hand(kind, p).wait_send()
        return 0

    lax.fori_loop(0, n // 2, drain_hands, 0)


def layer(queries, keys, values, seg_lengths, out_weight):
    rows, heads, hd = queries.shape
    n = lax.axis_size("ctx")
    marks = seg_lengths.shape[0]
    depth = out_weight.shape[0]
    cols = out_weight.shape[1] // 4
    by_head = lambda x: jnp.swapaxes(x, 0, 1)
    bf16, f32 = jnp.bfloat16, jnp.float32
    return pl.pallas_call(
        functools.partial(layer_kernel, n),
        out_shape=jax.ShapeDtypeStruct((rows, cols), bf16),
        in_specs=[pl.BlockSpec(memory_space=pltpu.VMEM)] * 4
        + [pl.BlockSpec(memory_space=pl.ANY)],
        out_specs=pl.BlockSpec(memory_space=pltpu.VMEM),
        scratch_shapes=[
            pltpu.VMEM((n, 2, marks, hd), bf16),
            pltpu.VMEM((n, 2, marks, hd), bf16),
            pltpu.VMEM((2, n, marks, hd), bf16),
            pltpu.VMEM((n, hd, marks), bf16),
            pltpu.VMEM((n, hd, marks), bf16),
            pltpu.VMEM((n, 8, marks), f32),
            pltpu.VMEM((n, 8, marks), f32),
            pltpu.VMEM((n, hd, marks), bf16),
            pltpu.VMEM((n, hd, marks), bf16),
            pltpu.VMEM((heads, rows, hd), f32),
            pltpu.VMEM((heads, rows, marks), bf16),
            pltpu.VMEM((rows, depth), bf16),
            pltpu.VMEM((4, depth, cols), bf16),
            pltpu.VMEM((2, depth, cols), bf16),
            pltpu.VMEM((rows, cols), bf16),
            pltpu.VMEM((rows, cols), bf16),
            pltpu.VMEM((rows, cols), bf16),
            pltpu.VMEM((rows, cols), bf16),
            pltpu.VMEM((rows, cols), bf16),
            pltpu.VMEM((rows, depth), bf16),
            pltpu.VMEM((rows, cols), bf16),
            pltpu.VMEM((rows, cols), bf16),
            pltpu.SemaphoreType.DMA((7, n)),
            pltpu.SemaphoreType.DMA((7, n)),
            pltpu.SemaphoreType.DMA((4,)),
            pltpu.SemaphoreType.DMA((8,)),
            pltpu.SemaphoreType.DMA((8,)),
            pltpu.SemaphoreType.DMA((5, CHUNKS)),
            pltpu.SemaphoreType.DMA((5, CHUNKS)),
        ],
        compiler_params=pltpu.CompilerParams(
            collective_id=0, has_side_effects=True, vmem_limit_bytes=56 << 20
        ),
        name="layer",
    )(
        by_head(queries), by_head(keys), by_head(values),
        seg_lengths[None, :], out_weight,
    )


def on_device_any(queries, keys, values, seg_lengths, out_weight):
    one_head_each = queries.shape[1] == lax.axis_size("ctx")
    body = layer if one_head_each and lax.axis_size("tp") == 4 else on_device
    return body(queries, keys, values, seg_lengths, out_weight)


def solution(mesh):
    in_specs = (
        P("ctx", "tp", None),
        P("ctx", "tp", None),
        P("ctx", "tp", None),
        P(),
        P("tp", None),
    )
    out_specs = P("ctx", "tp")
    return jax.shard_map(
        on_device_any, mesh=mesh, in_specs=in_specs, out_specs=out_specs, check_vma=False
    )
```

```python
import functools

import jax
import jax.numpy as jnp
from jax import lax
from jax.experimental import pallas as pl
from jax.experimental.pallas import tpu as pltpu
from jax.sharding import PartitionSpec as P

ITERS = 6


very_negative = -1e30


def prefix(shard, axis, combine, identity):
    peers, index = (lax.axis_size(axis), lax.axis_index(axis))
    everything = jax.tree.map(
        lambda part, kind: lax.all_gather(part.astype(kind), axis),
        shard,
        (jnp.bfloat16, jnp.bfloat16, jnp.bfloat16),
    )
    start = jax.tree.map(
        lambda part, zero: jnp.broadcast_to(jnp.asarray(zero, part.dtype), part.shape),
        shard,
        identity,
    )

    def lap(k, before):
        reached = k < index
        new = combine(
            before, jax.tree.map(lambda part, own: part[k].astype(own.dtype), everything, shard)
        )
        return jax.tree.map(lambda a, b: jnp.where(reached, a, b), new, before)

    return lax.fori_loop(0, peers, lap, start)


def merge_states(earlier, latter):
    top_peak = jnp.maximum(earlier[0], latter[0])
    first_factor = jnp.exp(earlier[0] - top_peak)
    second_factor = jnp.exp(latter[0] - top_peak)
    return (
        top_peak,
        earlier[1] * first_factor + latter[1] * second_factor,
        earlier[2] * first_factor[..., None] + latter[2] * second_factor[..., None],
    )


def masked_weights(scores, allowed):
    masked = jnp.where(allowed, scores, very_negative)
    top_score = jnp.max(masked, axis=-1, keepdims=True)
    expo = jnp.where(allowed, jnp.exp(masked - top_score), 0.0)
    return expo / jnp.maximum(jnp.sum(expo, axis=-1, keepdims=True), 1.0)


def newton_inverse(attention_kernel):
    highest = lax.Precision.HIGHEST
    row_sum = jnp.max(jnp.sum(attention_kernel, axis=2), axis=-1)
    col_sum = jnp.max(jnp.sum(attention_kernel, axis=1), axis=-1)
    approx = jnp.swapaxes(attention_kernel, 1, 2) / (row_sum * col_sum)[:, None, None]
    identity = jnp.eye(attention_kernel.shape[-1], dtype=jnp.float32)
    for iteration in range(ITERS):
        applied = jnp.einsum("hij,hjk->hik", attention_kernel, approx, precision=highest)
        factor = 7.0 * identity - applied
        factor = 15.0 * identity - jnp.einsum("hij,hjk->hik", applied, factor, precision=highest)
        factor = 13.0 * identity - jnp.einsum("hij,hjk->hik", applied, factor, precision=highest)
        approx = 0.25 * jnp.einsum("hij,hjk->hik", approx, factor, precision=highest)
    return approx


def on_device(queries, keys, values, seg_lengths, out_weight):
    row_count, heads_here, head_dim = queries.shape
    landmarks = seg_lengths.shape[0]
    score_scale_factor = head_dim ** (-0.5)
    block_start = lax.axis_index("ctx") * row_count
    seg_ends = jnp.cumsum(seg_lengths)
    seg_begins = seg_ends - seg_lengths
    position = block_start + jnp.arange(row_count, dtype=jnp.int32)
    block_member_mask = (
        (position[None, :] >= seg_begins[:, None]) & (position[None, :] < seg_ends[:, None])
    ).astype(jnp.bfloat16)
    query_block_sums = jnp.einsum(
        "na,abf->bnf", block_member_mask, queries, preferred_element_type=jnp.float32
    )
    key_block_sums = jnp.einsum(
        "na,abf->bnf", block_member_mask, keys, preferred_element_type=jnp.float32
    )
    query_block_sums, key_block_sums = (
        lax.psum(query_block_sums.astype(jnp.bfloat16), "ctx").astype(jnp.float32),
        lax.psum(key_block_sums.astype(jnp.bfloat16), "ctx").astype(jnp.float32),
    )
    seg_root = jnp.sqrt(seg_lengths.astype(jnp.float32))[None, :, None]
    landmark_query_rows = (query_block_sums / seg_root).astype(jnp.bfloat16)
    landmark_key_rows = (key_block_sums / seg_root).astype(jnp.bfloat16)
    state_score_matrix = (
        jnp.einsum("fcb,pfb->fcp", landmark_query_rows, keys, preferred_element_type=jnp.float32)
        * score_scale_factor
    )
    state_peak = jnp.max(state_score_matrix, axis=-1)
    state_exponent = jnp.exp(state_score_matrix - state_peak[..., None])
    state_total = jnp.sum(state_exponent, axis=-1)
    state_running_total = jnp.einsum(
        "ogq,qoc->ogc",
        state_exponent.astype(jnp.bfloat16),
        values,
        preferred_element_type=jnp.float32,
    )
    start_state = (
        jnp.full((heads_here, landmarks), very_negative, jnp.float32),
        jnp.zeros((heads_here, landmarks), jnp.float32),
        jnp.zeros((heads_here, landmarks, head_dim), jnp.float32),
    )
    in_peak, in_total, in_acc = prefix(
        (state_peak, state_total, state_running_total), "ctx", merge_states, start_state
    )
    attention_kernel = jax.nn.softmax(
        jnp.einsum(
            "slu,szu->slz",
            landmark_query_rows,
            landmark_key_rows,
            preferred_element_type=jnp.float32,
        )
        * score_scale_factor,
        axis=-1,
    )
    pseudo_inverse_matrix = newton_inverse(attention_kernel)
    causal = jnp.arange(row_count)[:, None] >= jnp.arange(row_count)[None, :]
    local_scores = (
        jnp.einsum("thd,uhd->htu", queries, keys, preferred_element_type=jnp.float32)
        * score_scale_factor
    )
    local_scores = jnp.where(causal[None], local_scores, very_negative)
    local_probs = jax.nn.softmax(local_scores, axis=-1).astype(jnp.bfloat16)
    local_block_output = jnp.einsum(
        "htu,uhd->thd", local_probs, values, preferred_element_type=jnp.float32
    )
    allowed = seg_ends <= block_start
    landmark_value_rows = jnp.where(
        allowed[None, :, None], in_acc / jnp.maximum(in_total, 1.0)[..., None], 0.0
    )
    blended_state = jnp.einsum(
        "bxz,bzl->bxl", pseudo_inverse_matrix, landmark_value_rows, precision=lax.Precision.HIGHEST
    ).astype(jnp.bfloat16)
    landmark_score_matrix = (
        jnp.einsum("byz,yfz->ybf", queries, landmark_key_rows, preferred_element_type=jnp.float32)
        * score_scale_factor
    )
    landmark_weight_matrix = masked_weights(landmark_score_matrix, allowed[None, None, :]).astype(
        jnp.bfloat16
    )
    land_out = jnp.einsum(
        "ecp,epy->cey", landmark_weight_matrix, blended_state, preferred_element_type=jnp.float32
    )
    landmark_attention_layer = (
        (local_block_output + land_out)
        .astype(jnp.bfloat16)
        .reshape(row_count, heads_here * head_dim)
    )
    partial_value = jnp.dot(
        landmark_attention_layer, out_weight, preferred_element_type=jnp.float32
    )
    return lax.psum_scatter(
        partial_value.astype(jnp.bfloat16), "tp", scatter_dimension=1, tiled=True
    )


MESH_ID = pl.DeviceIdType.MESH
HIGHEST = lax.Precision.HIGHEST
CHUNKS = 8
DEPTH = 3
NT = (((1,), (1,)), ((), ()))
TN = (((0,), (0,)), ((), ()))


def layer_kernel(
    n, q_ref, k_ref, v_ref, len_ref, w_hbm, out_ref,
    sum_out, sum_in, land, acc_out, acc_in, stat_out, stat_in,
    mix_out, mix_in, local, weights, att, w_own, w_outer,
    far_out, near_out, cross_out, own_out, outer_in, att_in, far_in, cross_in,
    send_sem, recv_sem, load_sem, wsend_sem, wrecv_sem, zsend_sem, zrecv_sem,
):
    heads, rows, hd = q_ref.shape
    marks = len_ref.shape[1]
    scale = hd ** (-0.5)
    me = lax.axis_index("ctx")
    f32, bf16 = jnp.float32, jnp.bfloat16

    def push(phase, src, dst, peer):
        return pltpu.make_async_remote_copy(
            src_ref=src, dst_ref=dst,
            send_sem=send_sem.at[phase, peer], recv_sem=recv_sem.at[phase, me],
            device_id={"ctx": peer}, device_id_type=MESH_ID,
        )

    def arrival(phase, src, dst, peer):
        return pltpu.make_async_remote_copy(
            src_ref=src, dst_ref=dst,
            send_sem=send_sem.at[phase, peer], recv_sem=recv_sem.at[phase, peer],
            device_id={"ctx": peer}, device_id_type=MESH_ID,
        )

    t = lax.axis_index("tp")
    side = t // 2
    near_end, far_end = 3 * side, 3 - 3 * side
    mid, cross = 1 + side, 2 - side
    is_end = (t == near_end)
    is_mid = (t == mid)
    cols = out_ref.shape[1]
    chunk = rows // CHUNKS

    loads = [
        pltpu.make_async_copy(
            w_hbm.at[:, pl.ds(j * cols, cols)], w_own.at[j], load_sem.at[j]
        )
        for j in range(4)
    ]
    for load in loads:
        load.start()

    core = lax.rem(me, 2)
    sibling = me + 1 - 2 * core
    part = w_hbm.shape[0] // 4
    axis_bit = (2, 4)

    def flipped(i, p):
        return p + axis_bit[i] - 2 * axis_bit[i] * lax.rem(p // axis_bit[i], 2)

    def quarter(i, p):
        q = 2 * lax.rem(p // axis_bit[i], 2) + lax.rem(p, 2)
        return pl.ds(pl.multiple_of(q * part, part), part)

    def weight_hop(i, column):
        return pltpu.make_async_remote_copy(
            src_ref=w_hbm.at[quarter(i, me), pl.ds(pl.multiple_of(column * cols, cols), cols)],
            dst_ref=w_outer.at[i, quarter(i, me)],
            send_sem=wsend_sem.at[i], recv_sem=wrecv_sem.at[i],
            device_id={"tp": mid}, device_id_type=MESH_ID,
        )

    def weight_share(i, step, owner, to):
        return pltpu.make_async_remote_copy(
            src_ref=w_outer.at[i, quarter(i, owner)], dst_ref=w_outer.at[i, quarter(i, owner)],
            send_sem=wsend_sem.at[2 * step + i], recv_sem=wrecv_sem.at[2 * step + i],
            device_id={"ctx": to}, device_id_type=MESH_ID,
        )

    def line_copy(kind, c, src, dst, to):
        at = pl.ds(c * chunk, chunk)
        return pltpu.make_async_remote_copy(
            src_ref=src.at[at], dst_ref=dst.at[at],
            send_sem=zsend_sem.at[kind, c], recv_sem=zrecv_sem.at[kind, c],
            device_id={"tp": to}, device_id_type=MESH_ID,
        )

    def project(dst, first, count, src, w, j, add=None):
        step = 256
        here = pl.ds(first, count)

        def tile(i, _):
            at = pl.ds(pl.multiple_of(i * step, step), step)
            y = jnp.dot(src[here], w[j, :, at], preferred_element_type=f32)
            if add is not None:
                y = y + add[here, at].astype(f32)
            dst[here, at] = y.astype(bf16)
            return 0

        lax.fori_loop(0, cols // step, tile, 0)

    barrier = pltpu.get_barrier_semaphore()

    @pl.when(is_end)
    def _():
        pl.semaphore_signal(barrier, inc=1, device_id={"tp": mid}, device_id_type=MESH_ID)

    @pl.when(is_mid)
    def _():
        pl.semaphore_signal(barrier, inc=1, device_id={"tp": near_end}, device_id_type=MESH_ID)
        pl.semaphore_signal(barrier, inc=1, device_id={"tp": cross}, device_id_type=MESH_ID)

    for o in range(1, n):
        pl.semaphore_signal(
            barrier, inc=1, device_id={"ctx": lax.rem(me + o, n)}, device_id_type=MESH_ID
        )

    low = lax.broadcasted_iota(jnp.int32, (marks, marks), 0)
    high = lax.broadcasted_iota(jnp.int32, (marks, marks), 1)
    len_row = len_ref[...].astype(f32)
    len_col = jnp.broadcast_to(len_row, (8, marks)).T[:, 0:1]
    ends_col = jnp.sum(jnp.where(high <= low, len_row, 0.0), axis=1, keepdims=True)
    ends_row = jnp.sum(jnp.where(low <= high, len_col, 0.0), axis=0, keepdims=True)
    begins_col = ends_col - len_col
    root_col = jnp.sqrt(len_col)
    position = (
        me * rows + lax.broadcasted_iota(jnp.int32, (marks, rows), 1)
    ).astype(f32)
    member = jnp.where(
        (position >= begins_col) & (position < ends_col), 1.0, 0.0
    ).astype(bf16)

    def block_sums(p):
        return (
            jnp.dot(member, q_ref[p], preferred_element_type=f32).astype(bf16),
            jnp.dot(member, k_ref[p], preferred_element_type=f32).astype(bf16),
        )

    @pl.when(is_end)
    def _():
        pl.semaphore_wait(barrier, n)

    @pl.when(is_mid)
    def _():
        pl.semaphore_wait(barrier, n + 1)

    @pl.when(is_end)
    def _():
        weight_hop(0, mid).start()
        weight_hop(1, cross).start()

    def twin(p):
        return p + 1 - 2 * lax.rem(p, 2)

    def hand(phase, src, dst, sent, landed):
        return pltpu.make_async_remote_copy(
            src_ref=src, dst_ref=dst,
            send_sem=send_sem.at[phase, sent], recv_sem=recv_sem.at[phase, landed],
            device_id={"ctx": sibling}, device_id_type=MESH_ID,
        )

    def send_twin(i, _):
        p = twin(lax.rem(me + 2 * i, n))
        sum_out[p, 0], sum_out[p, 1] = block_sums(p)
        hand(0, sum_out.at[p], sum_in.at[p], p, p).start()
        return 0

    def chip_sums(p):
        q_part, k_part = block_sums(p)
        hand(0, sum_out.at[p], sum_in.at[p], p, p).wait_recv()
        return (
            (q_part.astype(f32) + sum_in[p, 0].astype(f32)),
            (k_part.astype(f32) + sum_in[p, 1].astype(f32)),
        )

    def send_sums(i, _):
        p = lax.rem(me + 2 * i, n)
        q_part, k_part = chip_sums(p)
        sum_out[p, 0] = q_part.astype(bf16)
        sum_out[p, 1] = k_part.astype(bf16)
        push(5, sum_out.at[p], sum_in.at[sibling], p).start()
        return 0

    lax.fori_loop(1, n // 2, send_twin, 0)
    send_twin(0, 0)
    lax.fori_loop(1, n // 2, send_sums, 0)
    own_q, own_k = chip_sums(me)
    sum_out[me, 0] = own_q.astype(bf16)
    sum_out[me, 1] = own_k.astype(bf16)

    half = rows // 2
    low_t = lax.broadcasted_iota(jnp.int32, (half, half), 0)
    low_u = lax.broadcasted_iota(jnp.int32, (half, half), 1)
    diagonal = low_t >= low_u

    def local_head(h, _):
        q, k, v = q_ref[h], k_ref[h], v_ref[h]
        s0 = lax.dot_general(q[:half], k[:half], NT, preferred_element_type=f32) * scale
        s0 = jnp.where(diagonal, s0, very_negative)
        e0 = jnp.exp(s0 - jnp.max(s0, axis=1, keepdims=True))
        n0 = jnp.sum(e0, axis=1, keepdims=True)
        local[h, :half] = jnp.dot(e0.astype(bf16), v[:half], preferred_element_type=f32) / n0
        s1 = lax.dot_general(q[half:], k[:half], NT, preferred_element_type=f32) * scale
        s2 = lax.dot_general(q[half:], k[half:], NT, preferred_element_type=f32) * scale
        s2 = jnp.where(diagonal, s2, very_negative)
        top = jnp.maximum(
            jnp.max(s1, axis=1, keepdims=True), jnp.max(s2, axis=1, keepdims=True)
        )
        e1 = jnp.exp(s1 - top)
        e2 = jnp.exp(s2 - top)
        n1 = jnp.sum(e1, axis=1, keepdims=True) + jnp.sum(e2, axis=1, keepdims=True)
        local[h, half:] = (
            jnp.dot(e1.astype(bf16), v[:half], preferred_element_type=f32)
            + jnp.dot(e2.astype(bf16), v[half:], preferred_element_type=f32)
        ) / n1
        return 0

    lax.fori_loop(0, heads, local_head, 0)

    def wait_sums(i, total):
        p = lax.rem(me + 2 * i, n)
        slot = twin(p)
        arrival(5, sum_out.at[p], sum_in.at[slot], p).wait_recv()
        return (total[0] + sum_in[slot, 0].astype(f32), total[1] + sum_in[slot, 1].astype(f32))

    q_sum, k_sum = lax.fori_loop(
        1, n // 2, wait_sums, (sum_out[me, 0].astype(f32), sum_out[me, 1].astype(f32))
    )
    land_q = (q_sum / root_col).astype(bf16)
    land_k = (k_sum / root_col).astype(bf16)
    land[0, me] = land_q
    land[1, me] = land_k

    LAND = (1, 6)

    def land_push(kind, p):
        return push(LAND[kind], land.at[kind, me], land.at[kind, me], p)

    def land_hand(kind, p):
        return hand(LAND[kind], land.at[kind, p], land.at[kind, p], twin(p), p)

    for kind in range(2):
        for i in range(1, n // 2):
            land_push(kind, lax.rem(me + 2 * i, n)).start()
        land_hand(kind, me).start()

    def land_wait(kind, p):
        arrival(LAND[kind], land.at[kind, p], land.at[kind, p], p).wait_recv()

    def split(a):
        top = a.astype(bf16)
        return top, (a - top.astype(f32)).astype(bf16)

    def product(a, b):
        return (
            jnp.dot(a[0], b[1], preferred_element_type=f32)
            + jnp.dot(a[1], b[0], preferred_element_type=f32)
            + jnp.dot(a[0], b[0], preferred_element_type=f32)
        )

    scores = lax.dot_general(land_q, land_k, NT, preferred_element_type=f32) * scale
    expo = jnp.exp(scores - jnp.max(scores, axis=1, keepdims=True))
    kernel = expo / jnp.sum(expo, axis=1, keepdims=True)
    row_sum = jnp.max(jnp.sum(kernel, axis=1, keepdims=True), axis=0, keepdims=True)
    col_sum = jnp.max(jnp.sum(kernel, axis=0, keepdims=True), axis=1, keepdims=True)
    eye = jnp.where(low == high, 1.0, 0.0).astype(f32)

    kernel_parts = split(kernel)

    def newton(_, z):
        z_parts = split(z)
        kz = product(kernel_parts, z_parts)
        kz_parts = split(kz)
        f = 15.0 * eye - product(kz_parts, split(7.0 * eye - kz))
        f = 13.0 * eye - product(kz_parts, split(f))
        return 0.25 * product(z_parts, split(f))

    def block_state(p):
        st = lax.dot_general(k_ref[p], land[0, p], NT, preferred_element_type=f32) * scale
        peak = jnp.max(st, axis=0, keepdims=True)
        e = jnp.exp(st - peak)
        total = jnp.sum(e, axis=0, keepdims=True)
        acc = lax.dot_general(v_ref[p], e.astype(bf16), TN, preferred_element_type=f32)
        line = lax.broadcasted_iota(jnp.int32, (8, marks), 0)
        return acc.astype(bf16), jnp.where(line == 0, peak, total)

    def send_state(p):
        acc_out[p], stat_out[p] = block_state(p)
        push(2, acc_out.at[p], acc_in.at[me], p).start()
        push(3, stat_out.at[p], stat_in.at[me], p).start()

    own_acc, own_stat = block_state(me)
    acc_in[me] = own_acc
    stat_in[me] = own_stat
    early = lax.fori_loop(0, 2, newton, kernel.T / (row_sum * col_sum))

    def relay_q(i, _):
        p = lax.rem(me + 2 * i, n)
        land_wait(0, p)
        land_hand(0, p).start()
        return 0

    lax.fori_loop(1, n // 2, relay_q, 0)

    def near_states(i, _):
        send_state(lax.rem(me + 2 * i, n))
        return 0

    lax.fori_loop(1, n // 2, near_states, 0)

    def relay_k(i, _):
        p = lax.rem(me + 2 * i, n)
        land_wait(1, p)
        land_hand(1, p).start()
        return 0

    lax.fori_loop(1, n // 2, relay_k, 0)

    early = lax.fori_loop(2, 3, newton, early)

    def twin_states(i, _):
        p = twin(lax.rem(me + 2 * i, n))
        land_wait(0, p)
        send_state(p)
        return 0

    lax.fori_loop(1, n // 2, twin_states, 0)
    twin_states(0, 0)
    pinv = lax.fori_loop(3, ITERS, newton, early)

    def wait_k(i, _):
        land_wait(1, twin(lax.rem(me + 2 * i, n)))
        return 0

    lax.fori_loop(0, n // 2, wait_k, 0)

    allowed_here = ends_row <= (me * rows).astype(f32)

    def land_head(h, _):
        s = lax.dot_general(q_ref[h], land[1, h], NT, preferred_element_type=f32) * scale
        s = jnp.where(allowed_here, s, very_negative)
        e = jnp.where(allowed_here, jnp.exp(s - jnp.max(s, axis=1, keepdims=True)), 0.0)
        weights[h] = (e / jnp.maximum(jnp.sum(e, axis=1, keepdims=True), 1.0)).astype(bf16)
        return 0

    lax.fori_loop(0, heads, land_head, 0)

    def scan_block(b, carry):
        peak, total, acc = carry
        allowed = ends_row <= (b * rows).astype(f32)
        lv = jnp.where(allowed, acc / jnp.maximum(total, 1.0), 0.0)
        mixed = lax.dot_general(
            lv, pinv, NT, precision=HIGHEST, preferred_element_type=f32
        ).astype(bf16)

        @pl.when(b == me)
        def _():
            mix_in[me] = mixed

        @pl.when(b != me)
        def _():
            mix_out[b] = mixed
            push(4, mix_out.at[b], mix_in.at[me], b).start()
            arrival(2, acc_out.at[b], acc_in.at[b], b).wait_recv()
            arrival(3, stat_out.at[b], stat_in.at[b], b).wait_recv()

        stat = stat_in[b]
        new_peak, new_total = stat[0:1], stat[1:2]
        top = jnp.maximum(peak, new_peak)
        first = jnp.exp(peak - top)
        second = jnp.exp(new_peak - top)
        return (
            top,
            total * first + new_total * second,
            acc * first + acc_in[b].astype(f32) * second,
        )

    lax.fori_loop(
        0, n, scan_block,
        (
            jnp.full((1, marks), very_negative, f32),
            jnp.zeros((1, marks), f32),
            jnp.zeros((hd, marks), f32),
        ),
    )

    def finish(o, _):
        h = lax.rem(me + o, n)

        @pl.when(h != me)
        def _():
            arrival(4, mix_out.at[h], mix_in.at[h], h).wait_recv()

        land_out = lax.dot_general(weights[h], mix_in[h], NT, preferred_element_type=f32)
        at = pl.multiple_of(h * hd, hd)
        att[:, pl.ds(at, hd)] = (local[h] + land_out).astype(bf16)
        return 0

    lax.fori_loop(0, n, finish, 0)
    for load in loads:
        load.wait()

    @pl.when(is_end)
    def _():
        for c in range(CHUNKS):
            project(far_out, c * chunk, chunk, att, w_own, far_end)
            if c >= DEPTH:
                line_copy(0, c - DEPTH, far_out, outer_in, mid).wait_send()
            line_copy(0, c, far_out, outer_in, mid).start()
        project(own_out, 0, rows, att, w_own, t)
        for c in range(CHUNKS):
            if c < DEPTH:
                line_copy(0, CHUNKS - DEPTH + c, far_out, outer_in, mid).wait_send()
            else:
                line_copy(1, c - DEPTH, att, att_in, mid).wait_send()
            line_copy(1, c, att, att_in, mid).start()
        for c in range(CHUNKS):
            at = pl.ds(c * chunk, chunk)
            line_copy(4, c, near_out, outer_in, mid).wait_recv()
            out_ref[at] = (own_out[at].astype(f32) + outer_in[at].astype(f32)).astype(bf16)
        for c in range(CHUNKS - DEPTH, CHUNKS):
            line_copy(1, c, att, att_in, mid).wait_send()
        weight_hop(0, mid).wait_send()
        weight_hop(1, cross).wait_send()

    @pl.when(is_mid)
    def _():
        project(far_out, 0, rows, att, w_own, far_end)
        for i in range(2):
            weight_hop(i, mid).wait_recv()
            weight_share(i, 1, me, flipped(i, me)).start()
            weight_share(i, 2, me, sibling).start()

        def pass_near(c):
            at = pl.ds(c * chunk, chunk)
            line_copy(2, c, far_out, far_in, cross).wait_recv()
            near_out[at] = (near_out[at].astype(f32) + far_in[at].astype(f32)).astype(bf16)
            line_copy(4, c, near_out, outer_in, near_end).start()

        for c in range(CHUNKS):
            at = pl.ds(c * chunk, chunk)
            line_copy(0, c, far_out, outer_in, near_end).wait_recv()
            far_out[at] = (far_out[at].astype(f32) + outer_in[at].astype(f32)).astype(bf16)
            line_copy(2, c, far_out, far_in, cross).start()
            if c == 0:
                project(near_out, 0, rows, att, w_own, near_end)
            if c == 1:
                project(cross_out, 0, rows, att, w_own, cross)
            if c == 2:
                project(own_out, 0, rows, att, w_own, t)
            if c >= 1:
                pass_near(c - 1)
            if c == CHUNKS // 2:
                for i in range(2):
                    weight_share(i, 1, flipped(i, me), flipped(i, me)).wait_recv()
                    weight_share(i, 3, flipped(i, me), sibling).start()
        for i in range(2):
            weight_share(i, 2, sibling, sibling).wait_recv()
            weight_share(i, 3, flipped(i, sibling), sibling).wait_recv()
        for c in range(CHUNKS):
            line_copy(1, c, att, att_in, near_end).wait_recv()
            project(cross_out, c * chunk, chunk, att_in, w_outer, 1, cross_out)
            line_copy(3, c, cross_out, cross_in, cross).start()
            project(own_out, c * chunk, chunk, att_in, w_outer, 0, own_out)
            if c == 0:
                pass_near(CHUNKS - 1)
        for c in range(CHUNKS):
            at = pl.ds(c * chunk, chunk)
            line_copy(3, c, cross_out, cross_in, cross).wait_recv()
            out_ref[at] = (own_out[at].astype(f32) + cross_in[at].astype(f32)).astype(bf16)
        for i in range(2):
            weight_share(i, 1, me, flipped(i, me)).wait_send()
            weight_share(i, 2, me, sibling).wait_send()
            weight_share(i, 3, flipped(i, me), sibling).wait_send()
        for c in range(CHUNKS):
            line_copy(2, c, far_out, far_in, cross).wait_send()
            line_copy(3, c, cross_out, cross_in, cross).wait_send()
            line_copy(4, c, near_out, outer_in, near_end).wait_send()

    def drain(o, _):
        p = lax.rem(me + o, n)
        push(2, acc_out.at[p], acc_in.at[me], p).wait_send()
        push(3, stat_out.at[p], stat_in.at[me], p).wait_send()
        push(4, mix_out.at[p], mix_in.at[me], p).wait_send()
        return 0

    lax.fori_loop(1, n, drain, 0)

    def drain_pairs(i, _):
        p = lax.rem(me + 2 * i, n)
        push(5, sum_out.at[p], sum_in.at[sibling], p).wait_send()
        for kind in range(2):
            land_push(kind, p).wait_send()
        return 0

    lax.fori_loop(1, n // 2, drain_pairs, 0)

    def drain_hands(i, _):
        p = lax.rem(me + 2 * i, n)
        hand(0, sum_out.at[twin(p)], sum_in.at[twin(p)], twin(p), twin(p)).wait_send()
        for kind in range(2):
            land_hand(kind, p).wait_send()
        return 0

    lax.fori_loop(0, n // 2, drain_hands, 0)


def layer(queries, keys, values, seg_lengths, out_weight):
    rows, heads, hd = queries.shape
    n = lax.axis_size("ctx")
    marks = seg_lengths.shape[0]
    depth = out_weight.shape[0]
    cols = out_weight.shape[1] // 4
    by_head = lambda x: jnp.swapaxes(x, 0, 1)
    bf16, f32 = jnp.bfloat16, jnp.float32
    return pl.pallas_call(
        functools.partial(layer_kernel, n),
        out_shape=jax.ShapeDtypeStruct((rows, cols), bf16),
        in_specs=[pl.BlockSpec(memory_space=pltpu.VMEM)] * 4
        + [pl.BlockSpec(memory_space=pl.ANY)],
        out_specs=pl.BlockSpec(memory_space=pltpu.VMEM),
        scratch_shapes=[
            pltpu.VMEM((n, 2, marks, hd), bf16),
            pltpu.VMEM((n, 2, marks, hd), bf16),
            pltpu.VMEM((2, n, marks, hd), bf16),
            pltpu.VMEM((n, hd, marks), bf16),
            pltpu.VMEM((n, hd, marks), bf16),
            pltpu.VMEM((n, 8, marks), f32),
            pltpu.VMEM((n, 8, marks), f32),
            pltpu.VMEM((n, hd, marks), bf16),
            pltpu.VMEM((n, hd, marks), bf16),
            pltpu.VMEM((heads, rows, hd), f32),
            pltpu.VMEM((heads, rows, marks), bf16),
            pltpu.VMEM((rows, depth), bf16),
            pltpu.VMEM((4, depth, cols), bf16),
            pltpu.VMEM((2, depth, cols), bf16),
            pltpu.VMEM((rows, cols), bf16),
            pltpu.VMEM((rows, cols), bf16),
            pltpu.VMEM((rows, cols), bf16),
            pltpu.VMEM((rows, cols), bf16),
            pltpu.VMEM((rows, cols), bf16),
            pltpu.VMEM((rows, depth), bf16),
            pltpu.VMEM((rows, cols), bf16),
            pltpu.VMEM((rows, cols), bf16),
            pltpu.SemaphoreType.DMA((7, n)),
            pltpu.SemaphoreType.DMA((7, n)),
            pltpu.SemaphoreType.DMA((4,)),
            pltpu.SemaphoreType.DMA((8,)),
            pltpu.SemaphoreType.DMA((8,)),
            pltpu.SemaphoreType.DMA((5, CHUNKS)),
            pltpu.SemaphoreType.DMA((5, CHUNKS)),
        ],
        compiler_params=pltpu.CompilerParams(
            collective_id=0, has_side_effects=True, vmem_limit_bytes=56 << 20
        ),
        name="layer",
    )(
        by_head(queries), by_head(keys), by_head(values),
        seg_lengths[None, :], out_weight,
    )


def on_device_any(queries, keys, values, seg_lengths, out_weight):
    one_head_each = queries.shape[1] == lax.axis_size("ctx")
    body = layer if one_head_each and lax.axis_size("tp") == 4 else on_device
    return body(queries, keys, values, seg_lengths, out_weight)


def solution(mesh):
    in_specs = (
        P("ctx", "tp", None),
        P("ctx", "tp", None),
        P("ctx", "tp", None),
        P(),
        P("tp", None),
    )
    out_specs = P("ctx", "tp")
    return jax.shard_map(
        on_device_any, mesh=mesh, in_specs=in_specs, out_specs=out_specs, check_vma=False
    )
```
